32 devices in a mesh: fsdp: 8 (over y, x, core), tp: 4 (over z).
Axes of the slice: x: 2, y: 2, z: 4, core: 2. Of those that a mesh axis runs over, the one named last changes fastest.
Arguments:
- frames: bfloat16 [16384, 768], P(('fsdp', 'tp')), may hold values from -6 to 6
- segments: int32 [16, 1024], P('fsdp'), may hold values from 0 to 2, never falling along the last dimension, each value on 1 to 896 neighbouring positions
- w_qkv: bfloat16 [768, 3, 768], P('fsdp', None, 'tp'), may hold values from -0.21875 to 0.21875
- w_out: bfloat16 [768, 768], P('tp', 'fsdp'), may hold values from -1.5 to 1.5
- w_up: bfloat16 [768, 3072], P('fsdp', 'tp'), may hold values from -0.21875 to 0.21875
- w_down: bfloat16 [3072, 768], P('tp', 'fsdp'), may hold values from -0.109375 to 0.109375
- head_bias: bfloat16 [2, 768], P(None, ('tp', 'fsdp')), may hold values from -3 to 3
- up_bias: bfloat16 [3072], P(('tp', 'fsdp')), may hold values from -3 to 3
- ln_gains: bfloat16 [2, 768], P(None, ('fsdp', 'tp')), may hold values from 0.5 to 1.5
- shifts: bfloat16 [4, 768], P(None, ('fsdp', 'tp')), may hold values from -2.390625 to 2.390625
- cotangent: bfloat16 [16384, 768], P(('fsdp', 'tp')), may hold values from -6 to 6
Outputs:
- output: bfloat16 [16384, 768], P(('fsdp', 'tp'))
- d_frames: bfloat16 [16384, 768], P(('fsdp', 'tp'))
- d_w_qkv: float32 [768, 3, 768], P('fsdp', None, 'tp')
- d_w_out: float32 [768, 768], P('tp', 'fsdp')
- d_w_up: float32 [768, 3072], P('fsdp', 'tp')
- d_w_down: float32 [3072, 768], P('tp', 'fsdp')
- d_head_bias: float32 [2, 768], P(None, ('tp', 'fsdp'))
- d_up_bias: float32 [3072], P(('tp', 'fsdp'))
- d_ln_gains: float32 [2, 768], P(None, ('fsdp', 'tp'))
- d_shifts: float32 [4, 768], P(None, ('fsdp', 'tp'))
The draws below stay inside these ranges and needn't reach their ends.
Inputs may be any that keep to these rules, and one draw needn't show every extreme that they name: `segments`: clip numbers never fall along a sequence; each clip covers 1 to 896 frames, and some clip covers exactly that many.
All inputs are finite; a program needn't handle non-finite values.
Results may differ from the reference program's by a relative error of at most 0.017.
Values may be sent and summed in bfloat16 or wider, within the bound.
No kernel may reach another device: no remote copies, remote signals or barrier semaphores. Data moves between devices by JAX's collectives and lax.ppermute only.
A program may use at most 128 MiB of HBM per device.

```python
import math
import jax
import jax.numpy as jnp
import numpy as np
from jax import lax

D = 768
HEADS = 12
HEAD_DIM = 64
FF = 3072
SEQ_LEN = 1024
CLIPS = 3
SEQ_GRP = 2
SEQS = 16
TOKENS = 16384
N_FSDP = 8


def level_of(key, extent, shards, least, top_value):
    gain, own = 1.0, jax.random.fold_in(key, 6)
    for axis_at, blocks in shards:
        steps = jnp.exp(jax.random.uniform(jax.random.fold_in(own, axis_at), (blocks,), jnp.float32, least / len(shards), top_value / len(shards)))
        gain = gain * jnp.repeat(steps, extent[axis_at] // blocks).reshape([-1 if axis == axis_at else 1 for axis in range(len(extent))])
    return gain


def split_up(amount, total, reach, slope):
    weights = [(1 << 20) // math.isqrt(standing ** slope) + 1 for standing in range(2, amount + 1)]
    spare, holding = total - reach - (amount - 1), [1] * (amount - 1)
    while spare > 0:
        movable = [i for i in range(amount - 1) if holding[i] < reach]
        whole, budget = sum([weights[i] for i in movable]), spare
        for i in movable:
            addition = min(reach - holding[i], max(1, budget * weights[i] // whole), spare)
            holding[i] = holding[i] + addition
            spare = spare - addition
    return np.array([reach] + holding)


def ragged(key, amount, total, most, lean):
    if amount == 2:
        one = jax.random.randint(key, (), max(1, total - most), min(most, total - 1) + 1)
        return jnp.stack([one, total - one])
    lengths = jnp.asarray(split_up(amount, total, most, lean), jnp.int32)
    pairs = (amount - 1) // 2
    source_of, taker = lengths[1:1 + 2 * pairs:2], lengths[2:2 + 2 * pairs:2]
    margin = jnp.minimum(source_of - 1, most - taker)
    shifted = jax.random.randint(jax.random.fold_in(key, 1), (pairs,), 0, 1 << 20) % (margin + 1)
    lengths = lengths.at[1:1 + 2 * pairs:2].set(source_of - shifted).at[2:2 + 2 * pairs:2].set(taker + shifted)
    return lengths[jax.random.permutation(jax.random.fold_in(key, 2), amount)]


def centred(rng, dims, scale, reach, split=(), kind=jnp.bfloat16):
    loudness = level_of(rng, dims, split, -0.22, 0.18) if split else 1.0
    values = jax.random.normal(rng, dims, jnp.float32) * scale * loudness
    return jnp.minimum(jnp.maximum(values, -reach), reach).astype(kind)


def setup_inputs(seed: int = 0) -> dict:
    seeds = jax.random.split(jax.random.key(seed), 12)
    return {
        "frames": centred(seeds[0], (TOKENS, D), 1.0, 6.0, ((0, 32),)),
        "segments": jax.vmap(lambda own: jnp.searchsorted(jnp.cumsum(ragged(own, CLIPS, SEQ_LEN, SEQ_LEN * 7 // 8, 1)), jnp.arange(SEQ_LEN), side="right"))(jax.random.split(seeds[1], SEQS)).reshape((SEQS, SEQ_LEN)).astype(jnp.int32),
        "w_qkv": centred(seeds[2], (D, 3, D), D ** -0.5, 0.21875, ((0, 8), (2, 4))),
        "w_out": centred(seeds[3], (D, D), (D // 48) ** -0.5, 1.5, ((0, 4), (1, 8))),
        "w_up": centred(seeds[4], (D, FF), D ** -0.5, 0.21875, ((0, 8), (1, 4))),
        "w_down": centred(seeds[5], (FF, D), FF ** -0.5, 0.109375, ((0, 4), (1, 8))),
        "head_bias": centred(seeds[6], (2, D), 0.5, 3.0, ((1, 32),)),
        "up_bias": centred(seeds[7], (FF,), 0.5, 3.0, ((0, 32),)),
        "ln_gains": jnp.clip(1.0 + 0.1 * jax.random.normal(seeds[8], (2, D), jnp.float32), 0.5, 1.5).astype(jnp.bfloat16),
        "shifts": centred(seeds[9], (4, D), 0.4, 2.390625, ((1, 32),)),
        "cotangent": centred(seeds[10], (TOKENS, D), 1.0, 6.0, ((0, 32),)),
    }


@jax.custom_vjp
def low(v):
    return lax.optimization_barrier(v.astype(jnp.bfloat16)).astype(jnp.float32)

@jax.custom_vjp
def low_back(v):
    return v

def low_keep(v):
    return (low(v), None)

def low_pass(kept, grad):
    return (grad,)

def back_keep(v):
    return (v, None)

def back_low(kept, grad):
    return (low(grad),)
low.defvjp(low_keep, low_pass)
low_back.defvjp(back_keep, back_low)
HIGHEST = lax.Precision.HIGHEST
EPSILON = 1e-05
MASKED = -1000000000.0

def normalize(values, gain_row, shift_row):
    average = lax.optimization_barrier(jnp.mean(values, axis=-1, keepdims=True))
    centered = values - average
    spread = lax.optimization_barrier(jnp.mean(centered * centered, axis=-1, keepdims=True))
    return centered * lax.rsqrt(spread + EPSILON) * gain_row + shift_row

def attend_sequence(pieces):
    queries, keys_seq, values_seq, labels = pieces
    scores = jnp.einsum('qhd,khd->hqk', queries, keys_seq, precision=HIGHEST) * HEAD_DIM ** (-0.5)
    scores = low_back(scores)
    same_clip = labels[:, None] == labels[None, :]
    scores = jnp.where(same_clip[None], scores, MASKED)
    shares = low(jax.nn.softmax(scores, axis=-1))
    return jnp.einsum('hqk,khd->qhd', shares, values_seq, precision=HIGHEST)

def forward(frames, labels, w_qkv, w_out, w_up, w_down, head_bias, up_bias, ln_gains, shifts):
    row_count = frames.shape[0]
    normed_one = low(normalize(frames, ln_gains[0], shifts[0]))
    projected = jnp.einsum('rd,dce->rce', normed_one, w_qkv, precision=HIGHEST)
    queries = low_back(low(projected[:, 0] + head_bias[0]))
    keys_all = low_back(low(projected[:, 1]))
    values_all = low_back(low(projected[:, 2] + head_bias[1]))
    split_shape = (SEQ_GRP, SEQ_LEN, HEADS, HEAD_DIM)
    mixed_rows = lax.map(jax.checkpoint(attend_sequence), (queries.reshape(split_shape), keys_all.reshape(split_shape), values_all.reshape(split_shape), labels))
    mixed_rows = low_back(low(mixed_rows.reshape(row_count, D)))
    attended = low_back(jnp.dot(mixed_rows, w_out, precision=HIGHEST))
    middle = frames + attended + shifts[2]
    normed_two = low(normalize(middle, ln_gains[1], shifts[1]))
    up_values = low_back(jnp.dot(normed_two, w_up, precision=HIGHEST) + up_bias)
    activated = low(jax.nn.gelu(up_values, approximate=False))
    return middle + jnp.dot(activated, w_down, precision=HIGHEST) + shifts[3]

def reference(frames, segments, w_qkv, w_out, w_up, w_down, head_bias, up_bias, ln_gains, shifts, cotangent):
    params = tuple((member.astype(jnp.float32) for member in (w_qkv, w_out, w_up, w_down, head_bias, up_bias, ln_gains, shifts)))
    group_rows = SEQ_GRP * SEQ_LEN
    inputs = frames.astype(jnp.float32).reshape(N_FSDP, group_rows, D)
    seed_rows = cotangent.astype(jnp.float32).reshape(N_FSDP, group_rows, D)
    labels_all = segments.reshape(N_FSDP, SEQ_GRP, SEQ_LEN)

    def advance(totals, pieces):
        block_rows, block_labels, block_seed = pieces

        def apply_block(block_in, *weights):
            return forward(block_in, block_labels, *weights)
        result, pullback = jax.vjp(apply_block, block_rows, *params)
        gradients = pullback(block_seed)
        summed = tuple((older + incoming for older, incoming in zip(totals, gradients[1:])))
        return (summed, (result, gradients[0]))
    zeros_init = tuple((jnp.zeros_like(member) for member in params))
    totals, (results, d_rows) = lax.scan(advance, zeros_init, (inputs, labels_all, seed_rows))
    output = results.reshape(TOKENS, D).astype(jnp.bfloat16)
    d_frames = d_rows.reshape(TOKENS, D).astype(jnp.bfloat16)
    return (output, d_frames, totals[0], totals[1], totals[2], totals[3], totals[4], totals[5], totals[6], totals[7])
```

```python
import jax
import jax.numpy as jnp
from jax import lax
from jax.experimental import pallas as pl
from jax.experimental.pallas import tpu as pltpu
from jax.sharding import PartitionSpec as P

HEAD_DIM = 64
LANES = 128
CLIPS = 3
EPSILON = 1e-05
MASKED = -1000000000.0
LOW = jnp.bfloat16
FULL = jnp.float32


def normalize(values, gain_row, shift_row):
    average = jnp.mean(values, axis=-1, keepdims=True)
    centered = values - average
    inverse = lax.rsqrt(jnp.mean(centered * centered, axis=-1, keepdims=True) + EPSILON)
    normed = centered * inverse
    return (normed * gain_row + shift_row, normed, inverse)


def norm_back(incoming, normed, inverse, gain_row):
    scaled = incoming * gain_row
    return inverse * (
        scaled
        - jnp.mean(scaled, axis=-1, keepdims=True)
        - normed * jnp.mean(scaled * normed, axis=-1, keepdims=True)
    )


def gelu_slope(up_values):
    cumulative = 0.5 * (1.0 + lax.erf(up_values * 0.7071067811865476))
    density = jnp.exp(-0.5 * up_values * up_values) * 0.3989422804014327
    return cumulative + up_values * density


def contract(left, right, left_dim, right_dim):
    return lax.dot_general(
        left, right, (((left_dim,), (right_dim,)), ((), ())), preferred_element_type=FULL
    )


def pieces_of(column):
    high = column.astype(LOW)
    rest = column - high.astype(FULL)
    middle = rest.astype(LOW)
    low = (rest - middle.astype(FULL)).astype(LOW)
    return high, middle, low


def lane_of(rows):
    return lax.broadcasted_iota(jnp.int32, (rows, LANES), 1)


def widen(ref, start, rows):
    half = ref[:rows, start : start + HEAD_DIM]
    return jnp.concatenate([half, half], axis=1)


def attend_kernel(heads, rows, keys, p_ref, ext_q_ref, ext_k_ref, mixed_ref, ext_ref, q_buf, k_buf, v_buf):
    width = heads * HEAD_DIM
    lane_q = lane_of(rows)
    lane_k = lane_of(keys)
    for head in range(heads):
        at = head * HEAD_DIM
        q_buf[head] = jnp.where(
            lane_q < HEAD_DIM,
            (widen(p_ref, at, rows).astype(FULL) * HEAD_DIM**-0.5).astype(LOW),
            ext_q_ref[...],
        )
        k_buf[head] = jnp.where(lane_k < HEAD_DIM, widen(p_ref, width + at, keys), ext_k_ref[...])
        v_buf[head] = widen(p_ref, 2 * width + at, keys)
    for head in range(heads):
        scores = contract(q_buf[head], k_buf[head], 1, 1)
        highest = jnp.max(scores, axis=1, keepdims=True)
        weights = jnp.exp(scores - highest)
        total = jnp.sum(weights, axis=1, keepdims=True)
        mixed = contract(weights.astype(LOW), v_buf[head], 1, 0) / total
        mixed_ref[:, head * HEAD_DIM : (head + 1) * HEAD_DIM] = mixed[:, :HEAD_DIM].astype(LOW)
        high, middle, low = pieces_of(-(highest + jnp.log(total)))
        ext_ref[head] = jnp.where(
            lane_q == HEAD_DIM,
            high,
            jnp.where(
                lane_q == HEAD_DIM + 1,
                middle,
                jnp.where(lane_q == HEAD_DIM + 2, low, ext_q_ref[...]),
            ),
        )


def attend(projected, ext_q, ext_k, heads):
    rows, keys = ext_q.shape[0], ext_k.shape[0]

    def kernel(*refs):
        attend_kernel(heads, rows, keys, *refs)

    return pl.pallas_call(
        kernel,
        out_shape=(
            jax.ShapeDtypeStruct((rows, heads * HEAD_DIM), LOW),
            jax.ShapeDtypeStruct((heads, rows, LANES), LOW),
        ),
        scratch_shapes=[
            pltpu.VMEM((heads, rows, LANES), LOW),
            pltpu.VMEM((heads, keys, LANES), LOW),
            pltpu.VMEM((heads, keys, LANES), LOW),
        ],
        cost_estimate=pl.CostEstimate(
            flops=4 * heads * rows * keys * LANES,
            transcendentals=heads * rows * keys,
            bytes_accessed=2 * (projected.size + 2 * rows * heads * LANES),
        ),
        compiler_params=pltpu.CompilerParams(vmem_limit_bytes=40 << 20),
        name="attend",
    )(projected, ext_q, ext_k)


def back_kernel(
    heads, rows, keys, p_ref, up_ref, mixed_ref, ext_ref, ext_k_ref,
    dq_ref, own_ref, other_ref, q_buf, k_buf, v_buf, u_buf, dq_buf, dk_buf, dv_buf,
):
    width = heads * HEAD_DIM
    lane_q = lane_of(rows)
    lane_k = lane_of(keys)
    ext_k = ext_k_ref[...]
    for head in range(heads):
        at = head * HEAD_DIM
        q_buf[head] = jnp.where(
            lane_q < HEAD_DIM,
            (widen(p_ref, at, rows).astype(FULL) * HEAD_DIM**-0.5).astype(LOW),
            ext_ref[head],
        )
        k_buf[head] = jnp.where(lane_k < HEAD_DIM, widen(p_ref, width + at, keys), ext_k)
        v_buf[head] = jnp.where(lane_k < HEAD_DIM, widen(p_ref, 2 * width + at, keys), ext_k)
        upstream = widen(up_ref, at, rows)
        centre = 0.5 * jnp.sum(
            upstream.astype(FULL) * widen(mixed_ref, at, rows).astype(FULL), axis=1, keepdims=True
        )
        high, middle, low = pieces_of(-centre)
        u_buf[head] = jnp.where(
            lane_q < HEAD_DIM,
            upstream,
            jnp.where(
                lane_q == HEAD_DIM,
                high,
                jnp.where(
                    lane_q == HEAD_DIM + 1,
                    middle,
                    jnp.where(lane_q == HEAD_DIM + 2, low, jnp.zeros((), LOW)),
                ),
            ),
        )
    block = 256

    def one_head(head, carry):
        queries = q_buf[head]
        upstream = u_buf[head]
        total = jnp.zeros((rows, LANES), FULL)
        for start in range(0, keys, block):
            span = pl.ds(start, block)
            keys_part = k_buf[head, span, :]
            shares = jnp.exp(contract(keys_part, queries, 1, 1))
            d_scores = (shares * contract(v_buf[head, span, :], upstream, 1, 1)).astype(LOW)
            dv_buf[head, span, :] = contract(shares.astype(LOW), upstream, 1, 0)
            dk_buf[head, span, :] = contract(d_scores, queries, 1, 0)
            total = total + contract(d_scores, keys_part, 0, 0)
        dq_buf[head] = total * HEAD_DIM**-0.5
        return carry

    lax.fori_loop(0, heads, one_head, 0)
    for head in range(heads):
        at = head * HEAD_DIM
        dq_ref[:, at : at + HEAD_DIM] = dq_buf[head][:, :HEAD_DIM].astype(LOW)
        for buf, base in ((dk_buf, 0), (dv_buf, width)):
            own_ref[:, base + at : base + at + HEAD_DIM] = buf[head, :rows, :][:, :HEAD_DIM]
            other_ref[:, base + at : base + at + HEAD_DIM] = buf[head, rows:, :][
                :, :HEAD_DIM
            ].astype(LOW)


def attend_back(projected, upstream, mixed, ext, ext_k, heads):
    rows, keys = upstream.shape[0], ext_k.shape[0]
    width = heads * HEAD_DIM

    def kernel(*refs):
        back_kernel(heads, rows, keys, *refs)

    return pl.pallas_call(
        kernel,
        out_shape=(
            jax.ShapeDtypeStruct((rows, width), LOW),
            jax.ShapeDtypeStruct((rows, 2 * width), FULL),
            jax.ShapeDtypeStruct((keys - rows, 2 * width), LOW),
        ),
        scratch_shapes=[
            pltpu.VMEM((heads, rows, LANES), LOW),
            pltpu.VMEM((heads, keys, LANES), LOW),
            pltpu.VMEM((heads, keys, LANES), LOW),
            pltpu.VMEM((heads, rows, LANES), LOW),
            pltpu.VMEM((heads, rows, LANES), FULL),
            pltpu.VMEM((heads, keys, LANES), FULL),
            pltpu.VMEM((heads, keys, LANES), FULL),
        ],
        cost_estimate=pl.CostEstimate(
            flops=10 * heads * rows * keys * LANES,
            transcendentals=heads * rows * keys,
            bytes_accessed=2 * (projected.size + 6 * rows * heads * LANES),
        ),
        compiler_params=pltpu.CompilerParams(vmem_limit_bytes=40 << 20),
        name="attend_back",
    )(projected, upstream, mixed, ext, ext_k)


def build(fsdp, tp):
    bits = fsdp.bit_length() - 1
    masks = sorted(range(fsdp), key=lambda mask: (mask & 1, mask >> 1))

    def flip(array, bit):
        return lax.ppermute(array, "fsdp", [(at, at ^ (1 << bit)) for at in range(fsdp)])

    def flip_tp(array, bit):
        return lax.ppermute(array, "tp", [(at, at ^ (1 << bit)) for at in range(tp)])

    def ahead(array):
        return lax.ppermute(array, "tp", [(at, (at + 1) % tp) for at in range(tp)])

    def behind(array):
        return lax.ppermute(array, "tp", [(at, (at - 1) % tp) for at in range(tp)])

    def trade_rows(array):
        pairs = []
        for row in range(fsdp):
            for column in range(tp):
                odd = (row ^ column) & 1
                pairs.append((row * tp + column, (row ^ odd) * tp + (column ^ odd)))
        return lax.ppermute(array, ("fsdp", "tp"), pairs)

    def sum_everywhere(array):
        for bit in range(bits):
            array = array + flip(array, bit)
        for bit in range(tp.bit_length() - 1):
            array = array + flip_tp(array, bit)
        return array

    def order_of(slot):
        upper = list(range(1, bits))
        return upper if slot % 2 == 0 else upper[::-1]

    def gather_rows(shard, slot):
        rows = shard.shape[0]
        current, held = shard, [0]
        for bit in order_of(slot):
            arrived = flip(current, bit)
            both = held + [mask ^ (1 << bit) for mask in held]
            parts = [current, arrived]
            if bit == order_of(slot)[-1] and both != sorted(both):
                cut = [half[at * rows : (at + 1) * rows] for half in parts for at in range(len(held))]
                parts = [cut[both.index(mask)] for mask in sorted(both)]
                both = sorted(both)
            current, held = jnp.concatenate(parts, axis=0), both
        return jnp.concatenate([current, flip(current, 0)], axis=0)

    def scatter_rows(kept, sent, slot):
        current = kept + flip(sent, 0).astype(FULL)
        held = [mask for mask in masks if not mask & 1]
        rows = current.shape[0] // len(held)
        for bit in order_of(slot)[::-1]:
            stay = [at for at, mask in enumerate(held) if not mask >> bit & 1]
            leave = [at for at, mask in enumerate(held) if mask >> bit & 1]

            def pick(positions):
                if positions == list(range(positions[0], positions[0] + len(positions))):
                    return current[positions[0] * rows : (positions[-1] + 1) * rows]
                return jnp.concatenate([current[at * rows : (at + 1) * rows] for at in positions])

            current = pick(stay) + flip(pick(leave).astype(LOW), bit).astype(FULL)
            held = [held[at] for at in stay]
        return current

    def ring(shard):
        slots = [shard]
        for _ in range(tp - 1):
            slots.append(ahead(slots[-1]))
        return slots

    def local(
        frames, segments, w_qkv, w_out, w_up, w_down, head_bias, up_bias, ln_gains, shifts, cotangent
    ):
        row = lax.axis_index("fsdp")
        column = lax.axis_index("tp")
        rows, model = frames.shape
        block = model // fsdp
        width = w_qkv.shape[2]
        heads = width // HEAD_DIM
        units = w_up.shape[1]
        fine = ln_gains.shape[1]

        first = jnp.concatenate([w_qkv.reshape(block, 3 * width), w_out.T], axis=1)
        first_slots = [gather_rows(shard, slot) for slot, shard in enumerate(ring(first))]
        up_slots = [gather_rows(shard, slot) for slot, shard in enumerate(ring(w_up))]
        down_slots = [gather_rows(shard, slot) for slot, shard in enumerate(ring(w_down.T))]

        small = jnp.concatenate(
            [
                ln_gains.reshape(1, -1),
                shifts.reshape(1, -1),
                head_bias.reshape(1, -1),
                up_bias.reshape(1, -1),
            ],
            axis=1,
        )
        place = lax.broadcasted_iota(jnp.int32, (fsdp * tp, 1), 0) == row * tp + column
        small = sum_everywhere(jnp.where(place, small, jnp.zeros((), LOW)))
        cut = 6 * fine
        norm_rows = small[:, :cut].reshape(fsdp * tp, 6, fine).transpose(1, 0, 2).reshape(6, model)
        piece = head_bias.shape[1]
        head_rows = small[:, cut : cut + 2 * piece].reshape(fsdp, tp, 2, piece)
        head_rows = head_rows.transpose(1, 2, 0, 3).reshape(tp, 2, width).astype(FULL)
        up_rows = small[:, cut + 2 * piece :].reshape(fsdp, tp, up_bias.shape[0])
        up_rows = up_rows.transpose(1, 0, 2).reshape(tp, 1, units).astype(FULL)

        out_at = lax.broadcasted_iota(jnp.int32, (model, model), 1)
        in_at = lax.broadcasted_iota(jnp.int32, (model, model), 0)
        spot = out_at // block
        mask_at = ((spot & (fsdp // 2 - 1)) << 1) | (spot >> (bits - 1))
        shuffle = (in_at == (row ^ mask_at) * block + out_at % block).astype(LOW)

        def enter(array):
            return contract(array, shuffle, 1, 0)

        def leave(array):
            return trade_rows(contract(array, shuffle, 1, 1).astype(LOW))

        norm_rows = enter(norm_rows)
        gains_all, shifts_all = norm_rows[:2], norm_rows[2:]
        here = tp // segments.shape[0]
        labels = trade_rows(lax.dynamic_index_in_dim(segments, column // here, 0, keepdims=False))
        half = labels.shape[0] // here
        low_half, high_half = labels[:half], labels[half:]
        parity = row & 1
        own_labels = jnp.where(parity == 0, low_half, high_half)
        other_labels = jnp.where(parity == 0, high_half, low_half)
        all_labels = jnp.concatenate([own_labels, other_labels])

        def extension(labels_part, lead, marks):
            lane = lane_of(labels_part.shape[0])
            clip = lane - (HEAD_DIM + 3)
            values = jnp.where((clip >= 0) & (clip < CLIPS), marks(clip == labels_part[:, None]), 0.0)
            is_lead = (lane >= HEAD_DIM) & (lane < HEAD_DIM + 3)
            return jnp.where(is_lead, lead, values).astype(LOW)

        ext_q = extension(own_labels, 0.0, lambda same: jnp.where(same, 0.0, MASKED))
        ext_k = extension(all_labels, 1.0, lambda same: jnp.where(same, 1.0, 0.0))

        local_rows = enter(trade_rows(frames))
        upstream = enter(trade_rows(cotangent))
        upstream_low = upstream.astype(LOW)
        first_norm, unit_one, inverse_one = normalize(local_rows, gains_all[0], shifts_all[0])
        first_low = first_norm.astype(LOW)
        head_cut = model // 2
        arrived = flip(first_low, 0)
        arrived = jnp.concatenate([arrived[:, head_cut:], arrived[:, :head_cut]], axis=1)
        first_both = jnp.concatenate([first_low, arrived], axis=0)

        def slot_row(array, slot):
            return lax.dynamic_index_in_dim(array, (column - slot + tp) % tp, 0, keepdims=False)

        projected, mixed, extended = [], [], []
        for slot in range(tp):
            bias = slot_row(head_rows, slot)
            bias = jnp.concatenate([bias[0], jnp.zeros((width,), FULL), bias[1]])
            product = contract(first_both, first_slots[slot][:, : 3 * width], 1, 0) + bias
            projected.append(product.astype(LOW))
            answer, ext = attend(projected[slot], ext_q, ext_k, heads)
            mixed.append(answer)
            extended.append(ext)
        out_full = jnp.concatenate([part[:, 3 * width :] for part in first_slots], axis=1)
        mixed_all = jnp.concatenate(mixed, axis=1)
        middle = local_rows + contract(mixed_all, out_full, 1, 1) + shifts_all[2]
        second_norm, unit_two, inverse_two = normalize(middle, gains_all[1], shifts_all[1])
        second_low = second_norm.astype(LOW)

        up_values, activated = [], []
        mlp_out = jnp.zeros((rows, model), FULL)
        for slot in range(tp):
            values = contract(second_low, up_slots[slot], 1, 0) + slot_row(up_rows, slot)
            up_values.append(values)
            activated.append(jax.nn.gelu(values, approximate=False).astype(LOW))
        for slot in range(tp):
            mlp_out = mlp_out + contract(activated[slot], down_slots[slot], 1, 1)
        result = leave((middle + mlp_out + shifts_all[3]).astype(LOW))

        def weight_grad(left, right, slot):
            sent = contract(left[:, head_cut:], right, 0, 0).astype(LOW)
            kept = contract(left[:, :head_cut], right, 0, 0)
            return scatter_rows(kept, sent, slot)

        def ring_sum(parts):
            total = parts[-1]
            for part in parts[-2::-1]:
                total = part + behind(total.astype(LOW)).astype(FULL)
            return total

        backwards = range(tp - 1, -1, -1)
        grad_down = [None] * tp
        grad_up = [None] * tp
        d_ups = [None] * tp
        d_second = jnp.zeros((rows, model), FULL)
        for slot in backwards:
            grad_down[slot] = weight_grad(upstream_low, activated[slot], slot)
        for slot in backwards:
            d_active = contract(upstream_low, down_slots[slot], 1, 0)
            d_up = (d_active * gelu_slope(up_values[slot])).astype(LOW)
            d_ups[slot] = d_up
            grad_up[slot] = weight_grad(second_low, d_up, slot)
            d_second = d_second + contract(d_up, up_slots[slot], 1, 1)
        d_middle = upstream + norm_back(d_second, unit_two, inverse_two, gains_all[1])
        d_middle_low = d_middle.astype(LOW)
        d_mixed = contract(d_middle_low, out_full, 1, 0).astype(LOW)

        grad_first = [None] * tp
        d_first = jnp.zeros((rows, model), FULL)
        head_sums = [None] * tp
        for slot in backwards:
            d_answer = d_mixed[:, slot * width : (slot + 1) * width]
            d_query, own, other = attend_back(
                projected[slot], d_answer, mixed[slot], extended[slot], ext_k, heads
            )
            d_rest = (own + flip(other, 0).astype(FULL)).astype(LOW)
            d_all = jnp.concatenate([d_query, d_rest], axis=1)
            grad_first[slot] = scatter_rows(
                jnp.concatenate(
                    [
                        contract(first_low[:, :head_cut], d_all, 0, 0),
                        contract(d_middle_low[:, :head_cut], mixed[slot], 0, 0),
                    ],
                    axis=1,
                ),
                jnp.concatenate(
                    [
                        contract(first_low[:, head_cut:], d_all, 0, 0).astype(LOW),
                        contract(d_middle_low[:, head_cut:], mixed[slot], 0, 0).astype(LOW),
                    ],
                    axis=1,
                ),
                slot,
            )
            d_first = d_first + contract(d_all, first_slots[slot][:, : 3 * width], 1, 1)
            sums = jnp.sum(d_all.astype(FULL), axis=0)
            head_sums[slot] = jnp.stack([sums[:width], sums[2 * width :]])
        d_rows = d_middle + norm_back(d_first, unit_one, inverse_one, gains_all[0])

        def by_tp(parts):
            at = lax.broadcasted_iota(jnp.int32, (tp,) + (1,) * parts[0].ndim, 0)
            total = 0.0
            for slot, part in enumerate(parts):
                total = total + jnp.where(at == (column - slot + tp) % tp, part[None], 0.0)
            return total

        def back_order(sums):
            return lax.dot_general(
                sums,
                shuffle.astype(FULL),
                (((1,), (1,)), ((), ())),
                precision=lax.Precision.HIGHEST,
                preferred_element_type=FULL,
            )

        def column_sums(*arrays):
            return back_order(jnp.stack([jnp.sum(array, axis=0) for array in arrays]))

        early = column_sums(d_second * unit_two, d_second, d_middle, upstream)
        unit_sums = by_tp([jnp.sum(part.astype(FULL), axis=0) for part in d_ups])
        early = sum_everywhere(jnp.concatenate([early, unit_sums], axis=0) if units == model
                               else jnp.concatenate([early.reshape(-1), unit_sums.reshape(-1)]))
        early = early.reshape(-1)
        early, unit_sums = early[: 4 * model].reshape(4, model), early[4 * model :]
        late = column_sums(d_first * unit_one, d_first)
        head_part = by_tp(head_sums).transpose(1, 0, 2).reshape(2, tp * width)
        late = sum_everywhere(jnp.concatenate([late, head_part], axis=0))
        spot_model = (row * tp + column) * fine
        spot_units = column * fsdp + row

        def own_columns(array):
            return lax.dynamic_slice_in_dim(array, spot_model, fine, 1)

        gain_grads = own_columns(jnp.stack([late[0], early[0]]))
        shift_grads = own_columns(jnp.stack([late[1], early[1], early[2], early[3]]))
        grad_headbias = lax.dynamic_slice_in_dim(late[2:], spot_units * piece, piece, 1)
        grad_upbias = lax.dynamic_slice_in_dim(
            unit_sums, spot_units * up_bias.shape[0], up_bias.shape[0], 0
        )

        total_first = ring_sum(grad_first)
        total_up = ring_sum(grad_up)
        total_down = ring_sum(grad_down)
        return (
            result,
            leave(d_rows.astype(LOW)),
            total_first[:, : 3 * width].reshape(block, 3, width),
            total_first[:, 3 * width :].T,
            total_up,
            total_down.T,
            grad_headbias,
            grad_upbias,
            gain_grads,
            shift_grads,
        )

    return local


def solution(mesh):
    placed = (
        P(("fsdp", "tp"), None),
        P("fsdp", None),
        P("fsdp", None, "tp"),
        P("tp", "fsdp"),
        P("fsdp", "tp"),
        P("tp", "fsdp"),
        P(None, ("tp", "fsdp")),
        P(("tp", "fsdp")),
        P(None, ("fsdp", "tp")),
        P(None, ("fsdp", "tp")),
        P(("fsdp", "tp"), None),
    )
    return jax.shard_map(
        build(mesh.shape["fsdp"], mesh.shape["tp"]),
        mesh=mesh,
        in_specs=placed,
        out_specs=(
            P(("fsdp", "tp"), None),
            P(("fsdp", "tp"), None),
            P("fsdp", None, "tp"),
            P("tp", "fsdp"),
            P("fsdp", "tp"),
            P("tp", "fsdp"),
            P(None, ("tp", "fsdp")),
            P(("tp", "fsdp")),
            P(None, ("fsdp", "tp")),
            P(None, ("fsdp", "tp")),
        ),
        check_vma=False,
    )
```

```python
import jax
import jax.numpy as jnp
from jax import lax
from jax.experimental import pallas as pl
from jax.experimental.pallas import tpu as pltpu
from jax.sharding import PartitionSpec as P


HEAD_DIM = 64
LANES = 128
CLIPS = 3
EPSILON = 1e-05
MASKED = -1000000000.0
LOW = jnp.bfloat16
FULL = jnp.float32


def normalize(values, gain_row, shift_row):
    average = jnp.mean(values, axis=-1, keepdims=True)
    centered = values - average
    inverse = lax.rsqrt(jnp.mean(centered * centered, axis=-1, keepdims=True) + EPSILON)
    normed = centered * inverse
    return (normed * gain_row + shift_row, normed, inverse)


def norm_back(incoming, normed, inverse, gain_row):
    scaled = incoming * gain_row
    return inverse * (
        scaled
        - jnp.mean(scaled, axis=-1, keepdims=True)
        - normed * jnp.mean(scaled * normed, axis=-1, keepdims=True)
    )


def contract(left, right, left_dim, right_dim):
    return lax.dot_general(
        left, right, (((left_dim,), (right_dim,)), ((), ())), preferred_element_type=FULL
    )


def pieces_of(column):
    high = column.astype(LOW)
    rest = column - high.astype(FULL)
    middle = rest.astype(LOW)
    low = (rest - middle.astype(FULL)).astype(LOW)
    return high, middle, low


def lane_of(rows):
    return lax.broadcasted_iota(jnp.int32, (rows, LANES), 1)


def spread(ref_value, start):
    half = ref_value[:, start : start + HEAD_DIM]
    return jnp.concatenate([half, half], axis=1)


def put_pieces(lane, base, pieces, rest):
    for step, piece in enumerate(pieces):
        rest = jnp.where(lane == base + step, piece, rest)
    return rest


ANYWHERE = pl.BlockSpec(memory_space=pltpu.HBM)
WHOLE = pl.BlockSpec(memory_space=pltpu.VMEM)


def run_copies(moves, semaphores):
    copies = [
        pltpu.make_async_copy(source, target, semaphores.at[at])
        for at, (source, target) in enumerate(moves)
    ]
    for copy in copies:
        copy.start()
    for copy in copies:
        copy.wait()


def fetch(pieces, refs, target, semaphores):
    run_copies(
        [
            (refs[source].at[pl.ds(start, count)], target.at[pl.ds(put, count)])
            for source, start, put, count in pieces
        ],
        semaphores,
    )


def join(arrays):
    rows, columns = arrays[0].shape
    if rows % 16:
        return jnp.concatenate(arrays, axis=0)
    count = len(arrays)

    def kernel(*refs):
        for at in range(count):
            refs[count][at * rows : (at + 1) * rows, :] = refs[at][...]

    return pl.pallas_call(
        kernel,
        out_shape=jax.ShapeDtypeStruct((count * rows, columns), arrays[0].dtype),
        cost_estimate=pl.CostEstimate(
            flops=0, transcendentals=0, bytes_accessed=4 * count * rows * columns
        ),
        name="join",
    )(*arrays)


def attend_kernel(
    heads, rows, keys, pieces, normed_ref, bias_ref, ext_q_ref, ext_k_ref, acc_ref, *refs
):
    out_ref, mixed_out, q_out, k_out, v_out = refs[-12:-7]
    weight, mixed_ref, q_ref, k_ref, v_ref, semaphores, leaving = refs[-7:]
    width = heads * HEAD_DIM
    fetch(pieces, refs, weight, semaphores)
    lane_q = lane_of(rows)
    lane_k = lane_of(keys)
    ext_k = ext_k_ref[...]
    pair = contract(normed_ref[...], weight[:, : 2 * width], 1, 0) + bias_ref[:, : 2 * width]
    pair = pair.astype(LOW)
    query = contract(normed_ref[:rows, :], weight[:, 2 * width :], 1, 0) + bias_ref[:, 2 * width :]
    query = (query.astype(LOW).astype(FULL) * HEAD_DIM**-0.5).astype(LOW)
    for head in range(heads):
        at = head * HEAD_DIM
        q_ref[head] = jnp.where(lane_q < HEAD_DIM, spread(query, width + at), ext_q_ref[...])
        k_ref[head] = jnp.where(lane_k < HEAD_DIM, spread(pair, at), ext_k)
        v_ref[head] = jnp.where(lane_k < HEAD_DIM, spread(pair, width + at), ext_k)
    saves = [
        pltpu.make_async_copy(source, target, leaving.at[at])
        for at, (source, target) in enumerate(
            ((k_ref, k_out), (v_ref, v_out), (q_ref, q_out), (mixed_ref, mixed_out))
        )
    ]
    saves[0].start()
    saves[1].start()
    for head in range(heads):
        scores = contract(q_ref[head], k_ref[head], 1, 1)
        highest = jnp.max(scores, axis=1, keepdims=True)
        weights = jnp.exp(scores - highest)
        total = jnp.sum(weights, axis=1, keepdims=True)
        mixed = contract(weights.astype(LOW), v_ref[head], 1, 0) / total
        mixed_ref[:, head * HEAD_DIM : (head + 1) * HEAD_DIM] = mixed[:, :HEAD_DIM].astype(LOW)
        pieces = pieces_of(-(highest + jnp.log(total)))
        q_ref[head] = put_pieces(lane_q, HEAD_DIM, pieces, q_ref[head])
    saves[2].start()
    saves[3].start()
    out_ref[...] = acc_ref[...] + contract(mixed_ref[...], weight[:, 2 * width : 3 * width], 1, 1)
    for save in saves:
        save.wait()


def attend(normed, source, bias, ext_q, ext_k, acc, heads):
    arrays, pieces = source
    rows, keys = ext_q.shape[0], ext_k.shape[0]
    model = normed.shape[1]
    saved = [
        ((rows, heads * HEAD_DIM), LOW),
        ((heads, rows, LANES), LOW),
        ((heads, keys, LANES), LOW),
        ((heads, keys, LANES), LOW),
    ]

    def kernel(*refs):
        attend_kernel(heads, rows, keys, pieces, *refs)

    return pl.pallas_call(
        kernel,
        out_shape=(
            jax.ShapeDtypeStruct(acc.shape, FULL),
            *(jax.ShapeDtypeStruct(*item) for item in saved),
        ),
        in_specs=[WHOLE] * 5 + [ANYWHERE] * len(arrays),
        out_specs=(WHOLE,) + (ANYWHERE,) * 4,
        input_output_aliases={4: 0},
        scratch_shapes=[
            pltpu.VMEM((model, arrays[0].shape[1]), LOW),
            *(pltpu.VMEM(*item) for item in saved),
            pltpu.SemaphoreType.DMA((len(pieces),)),
            pltpu.SemaphoreType.DMA((4,)),
        ],
        cost_estimate=pl.CostEstimate(
            flops=4 * heads * rows * keys * LANES + 8 * rows * model * heads * HEAD_DIM,
            transcendentals=heads * rows * keys,
            bytes_accessed=2 * (normed.size + 4 * rows * model + 8 * rows * heads * LANES),
        ),
        compiler_params=pltpu.CompilerParams(vmem_limit_bytes=44 << 20),
        name="attend",
    )(normed, bias, ext_q, ext_k, acc, *arrays)


def mlp_kernel(
    block, pieces, place,
    normed_ref, normed_t_ref, seed_ref, seed_t_ref, bias_ref, out_in_ref, d_in_ref, *refs
):
    out_ref, d_ref, kept_out, sent_out, sums_ref = refs[-10:-5]
    weight, kept_ref, sent_ref, semaphores, leaving = refs[-5:]
    cut = kept_ref.shape[0]
    units = bias_ref.shape[1]

    def spans(at):
        return (
            pl.ds(pl.multiple_of(at * block, block), block),
            pl.ds(pl.multiple_of(units + at * block, block), block),
        )

    def copies(at):
        return [
            pltpu.make_async_copy(
                refs[source].at[pl.ds(start, count), span],
                weight.at[pl.ds(put, count), span],
                semaphores.at[at, 2 * order + side],
            )
            for order, (source, start, put, count) in enumerate(pieces)
            for side, span in enumerate(spans(at))
        ]

    def saves(at):
        return [
            pltpu.make_async_copy(
                source.at[:, span], target.at[place, :, span], leaving.at[at, 2 * order + side]
            )
            for order, (source, target) in enumerate(((kept_ref, kept_out), (sent_ref, sent_out)))
            for side, span in enumerate(spans(at))
        ]

    for at in range(units // block):
        for copy in copies(at):
            copy.start()
    out_ref[...] = out_in_ref[...]
    d_ref[...] = d_in_ref[...]

    def step(at, carry):
        span_up, span_down = spans(at)
        for copy in copies(at):
            copy.wait()
        up = contract(normed_ref[...], weight[:, span_up], 1, 0) + bias_ref[:, span_up]
        d_active = contract(seed_ref[...], weight[:, span_down], 1, 0)
        cumulative = 0.5 + 0.5 * lax.erf(up * 0.7071067811865476)
        active = (up * cumulative).astype(LOW)
        slope = cumulative + up * (jnp.exp(-0.5 * up * up) * 0.3989422804014327)
        d_up = (d_active * slope).astype(LOW)
        sums_ref[:, span_up] = jnp.sum(d_up.astype(FULL), axis=0, keepdims=True)
        out_ref[...] += contract(active, weight[:, span_down], 1, 1)
        d_ref[...] += contract(d_up, weight[:, span_up], 1, 1)
        grad_up = contract(normed_t_ref[...], d_up, 1, 0).astype(LOW)
        kept_ref[:, span_up] = grad_up[:cut]
        sent_ref[:, span_up] = grad_up[cut:]
        grad_down = contract(seed_t_ref[...], active, 1, 0).astype(LOW)
        kept_ref[:, span_down] = grad_down[:cut]
        sent_ref[:, span_down] = grad_down[cut:]
        for save in saves(at):
            save.start()
        return carry

    lax.fori_loop(0, units // block, step, 0)
    for at in range(units // block):
        for save in saves(at):
            save.wait()


def mlp(normed, normed_t, seed, seed_t, source, bias, out, d_normed, grads, at, total):
    arrays, pieces = source
    rows, model = normed.shape
    units = bias.shape[1]
    cut = model // 2

    def kernel(*refs):
        mlp_kernel(256, pieces, at, *refs)

    grad_shape = jax.ShapeDtypeStruct((total, cut, 2 * units), LOW)
    grads = list(grads)
    first = 7 + len(arrays)
    return pl.pallas_call(
        kernel,
        out_shape=(
            jax.ShapeDtypeStruct(out.shape, FULL),
            jax.ShapeDtypeStruct(out.shape, FULL),
            grad_shape,
            grad_shape,
            jax.ShapeDtypeStruct((1, units), FULL),
        ),
        in_specs=[WHOLE] * 7 + [ANYWHERE] * (len(arrays) + len(grads)),
        out_specs=(WHOLE, WHOLE, ANYWHERE, ANYWHERE, WHOLE),
        input_output_aliases={5: 0, 6: 1, **({first: 2, first + 1: 3} if grads else {})},
        scratch_shapes=[
            pltpu.VMEM((model, 2 * units), LOW),
            pltpu.VMEM((cut, 2 * units), LOW),
            pltpu.VMEM((cut, 2 * units), LOW),
            pltpu.SemaphoreType.DMA((units // 256, 2 * len(pieces))),
            pltpu.SemaphoreType.DMA((units // 256, 4)),
        ],
        cost_estimate=pl.CostEstimate(
            flops=12 * rows * model * units,
            transcendentals=2 * rows * units,
            bytes_accessed=16 * rows * model + 8 * model * units,
        ),
        compiler_params=pltpu.CompilerParams(vmem_limit_bytes=44 << 20),
        name="mlp",
    )(normed, normed_t, seed, seed_t, bias, out, d_normed, *arrays, *grads)


def back_kernel(
    heads, rows, keys, pieces,
    d_ref, d_t_ref, normed_t_ref, own_in_ref, other_in_ref, q_in, k_in, v_in, mixed_in, *refs
):
    own_ref, other_ref, kept_out, sent_out, sums_ref = refs[-19:-14]
    (
        weight, q_ref, k_ref, v_ref, mixed_ref, kept_ref, sent_ref,
        u_buf, dq_buf, dk_buf, dv_buf, pair_buf, query_buf, semaphores,
    ) = refs[-14:]
    width = heads * HEAD_DIM
    cut = kept_ref.shape[0]
    first = len(pieces)
    entering = [
        pltpu.make_async_copy(source, target, semaphores.at[first + at])
        for at, (source, target) in enumerate(
            ((mixed_in, mixed_ref), (q_in, q_ref), (k_in, k_ref), (v_in, v_ref))
        )
    ]
    for copy in entering:
        copy.start()
    fetch(pieces, refs, weight, semaphores)
    lane_q = lane_of(rows)
    upstream_all = contract(d_ref[...], weight[:, 2 * width : 3 * width], 1, 0).astype(LOW)
    entering[0].wait()
    mixed = mixed_ref[...]
    for head in range(heads):
        at = head * HEAD_DIM
        product = upstream_all[:, at : at + HEAD_DIM].astype(FULL) * mixed[
            :, at : at + HEAD_DIM
        ].astype(FULL)
        pieces_here = pieces_of(-jnp.sum(product, axis=1, keepdims=True))
        rest = jnp.where(lane_q < HEAD_DIM, spread(upstream_all, at), jnp.zeros((), LOW))
        u_buf[head] = put_pieces(lane_q, HEAD_DIM, pieces_here, rest)
    for copy in entering[1:]:
        copy.wait()
    block = 256

    def one_head(head, carry):
        queries = q_ref[head]
        upstream = u_buf[head]
        total = jnp.zeros((rows, LANES), FULL)
        for start in range(0, keys, block):
            span = pl.ds(start, block)
            keys_part = k_ref[head, span, :]
            shares = jnp.exp(contract(keys_part, queries, 1, 1))
            d_scores = (shares * contract(v_ref[head, span, :], upstream, 1, 1)).astype(LOW)
            dv_buf[head, span, :] = contract(shares.astype(LOW), upstream, 1, 0).astype(LOW)
            dk_buf[head, span, :] = contract(d_scores, queries, 1, 0).astype(LOW)
            total = total + contract(d_scores, keys_part, 0, 0)
        dq_buf[head] = (total * HEAD_DIM**-0.5).astype(LOW)
        return carry

    lax.fori_loop(0, heads, one_head, 0)
    query_buf[:, :width] = jnp.zeros((rows, width), LOW)
    for head in range(heads):
        at = head * HEAD_DIM
        query_buf[:, width + at : width + at + HEAD_DIM] = dq_buf[head][:, :HEAD_DIM]
        pair_buf[:, at : at + HEAD_DIM] = dk_buf[head][:, :HEAD_DIM]
        pair_buf[:, width + at : width + at + HEAD_DIM] = dv_buf[head][:, :HEAD_DIM]
    grad_pair = contract(normed_t_ref[...], pair_buf[...], 1, 0).astype(LOW)
    kept_ref[:, : 2 * width] = grad_pair[:cut]
    sent_ref[:, : 2 * width] = grad_pair[cut:]
    grad_query = contract(normed_t_ref[:, :rows], query_buf[...], 1, 0).astype(LOW)
    kept_ref[:, 2 * width :] = grad_query[:cut]
    sent_ref[:, 2 * width :] = grad_query[cut:]
    grad_out = contract(d_t_ref[...], mixed, 1, 0).astype(LOW)
    kept_ref[:, 2 * width : 3 * width] = grad_out[:cut]
    sent_ref[:, 2 * width : 3 * width] = grad_out[cut:]
    saves = [
        pltpu.make_async_copy(kept_ref, kept_out, semaphores.at[first + 4]),
        pltpu.make_async_copy(sent_ref, sent_out, semaphores.at[first + 5]),
    ]
    for save in saves:
        save.start()
    sums_ref[:, : 2 * width] = jnp.sum(pair_buf[...].astype(FULL), axis=0, keepdims=True)
    sums_ref[:, 2 * width :] = jnp.sum(query_buf[...].astype(FULL), axis=0, keepdims=True)
    own_ref[...] = (
        own_in_ref[...]
        + contract(pair_buf[:rows, :], weight[:, : 2 * width], 1, 1)
        + contract(query_buf[...], weight[:, 2 * width :], 1, 1)
    )
    other_ref[...] = other_in_ref[...] + contract(
        pair_buf[rows:, :], weight[:, : 2 * width], 1, 1
    )
    for save in saves:
        save.wait()


def attend_back(d_middle, d_middle_t, normed_t, source, saved, own, other, heads):
    arrays, pieces = source
    mixed, queries, keys_all, values = saved
    rows, keys = d_middle.shape[0], normed_t.shape[1]
    model = normed_t.shape[0]
    cut, columns = model // 2, arrays[0].shape[1]
    width = heads * HEAD_DIM

    def kernel(*refs):
        back_kernel(heads, rows, keys, pieces, *refs)

    return pl.pallas_call(
        kernel,
        out_shape=(
            jax.ShapeDtypeStruct(own.shape, FULL),
            jax.ShapeDtypeStruct(other.shape, FULL),
            jax.ShapeDtypeStruct((cut, columns), LOW),
            jax.ShapeDtypeStruct((cut, columns), LOW),
            jax.ShapeDtypeStruct((1, columns), FULL),
        ),
        in_specs=[WHOLE] * 5 + [ANYWHERE] * (4 + len(arrays)),
        out_specs=(WHOLE, WHOLE, ANYWHERE, ANYWHERE, WHOLE),
        input_output_aliases={3: 0, 4: 1},
        scratch_shapes=[
            pltpu.VMEM((model, columns), LOW),
            pltpu.VMEM((heads, rows, LANES), LOW),
            pltpu.VMEM((heads, keys, LANES), LOW),
            pltpu.VMEM((heads, keys, LANES), LOW),
            pltpu.VMEM((rows, width), LOW),
            pltpu.VMEM((cut, columns), LOW),
            pltpu.VMEM((cut, columns), LOW),
            pltpu.VMEM((heads, rows, LANES), LOW),
            pltpu.VMEM((heads, rows, LANES), LOW),
            pltpu.VMEM((heads, keys, LANES), LOW),
            pltpu.VMEM((heads, keys, LANES), LOW),
            pltpu.VMEM((keys, 2 * width), LOW),
            pltpu.VMEM((rows, columns - 2 * width), LOW),
            pltpu.SemaphoreType.DMA((len(pieces) + 6,)),
        ],
        cost_estimate=pl.CostEstimate(
            flops=10 * heads * rows * keys * LANES + 20 * rows * model * width,
            transcendentals=heads * rows * keys,
            bytes_accessed=8 * keys * model + 8 * rows * model,
        ),
        compiler_params=pltpu.CompilerParams(vmem_limit_bytes=44 << 20),
        name="attend_back",
    )(
        d_middle, d_middle_t, normed_t, own, other, queries, keys_all, values, mixed, *arrays
    )


def call_rows(kernel, shapes, *arrays):
    return pl.pallas_call(
        kernel,
        out_shape=tuple(jax.ShapeDtypeStruct(*shape) for shape in shapes),
        cost_estimate=pl.CostEstimate(
            flops=2 * arrays[0].size * arrays[0].shape[1],
            transcendentals=0,
            bytes_accessed=sum(array.size * array.dtype.itemsize for array in arrays),
        ),
        compiler_params=pltpu.CompilerParams(vmem_limit_bytes=44 << 20),
    )(*arrays)


def enter_kernel(rows_ref, shuffle_ref, out_ref, out_t_ref):
    moved = contract(rows_ref[...], shuffle_ref[...], 1, 0).astype(LOW)
    out_ref[...] = moved
    out_t_ref[...] = moved.T


def first_norm_kernel(rows_ref, shuffle_ref, norm_ref, rows_out, normed_ref):
    moved = contract(rows_ref[...], shuffle_ref[...], 1, 0)
    rows_out[...] = moved.astype(LOW)
    normed_ref[...] = normalize(moved, norm_ref[0:1, :], norm_ref[2:3, :])[0].astype(LOW)


def both_kernel(own_ref, other_ref, both_ref, both_t_ref):
    rows, model = own_ref.shape
    cut = model // 2
    both_ref[:rows, :] = own_ref[...]
    both_ref[rows:, :cut] = other_ref[:, cut:]
    both_ref[rows:, cut:] = other_ref[:, :cut]
    both_t_ref[...] = both_ref[...].T


def second_norm_kernel(rows_ref, attended_ref, norm_ref, middle_ref, normed_ref, normed_t_ref):
    middle = rows_ref[...].astype(FULL) + attended_ref[...] + norm_ref[4:5, :]
    middle_ref[...] = middle
    normed = normalize(middle, norm_ref[1:2, :], norm_ref[3:4, :])[0].astype(LOW)
    normed_ref[...] = normed
    normed_t_ref[...] = normed.T


def add_up(array):
    return jnp.sum(array, axis=0, keepdims=True)


def second_back_kernel(
    middle_ref, d_normed_ref, seed_ref, mlp_ref, norm_ref, shuffle_ref,
    d_ref, d_low_ref, d_t_ref, result_ref, sums_ref,
):
    middle = middle_ref[...]
    _, unit, inverse = normalize(middle, norm_ref[1:2, :], norm_ref[3:4, :])
    d_normed = d_normed_ref[...]
    seed = seed_ref[...].astype(FULL)
    d_middle = seed + norm_back(d_normed, unit, inverse, norm_ref[1:2, :])
    d_ref[...] = d_middle
    low = d_middle.astype(LOW)
    d_low_ref[...] = low
    d_t_ref[...] = low.T
    sums_ref[0:1, :] = add_up(d_normed * unit)
    sums_ref[1:2, :] = add_up(d_normed)
    sums_ref[2:3, :] = add_up(d_middle)
    sums_ref[3:4, :] = add_up(seed)
    result = (middle + mlp_ref[...] + norm_ref[5:6, :]).astype(LOW)
    result_ref[...] = contract(result, shuffle_ref[...], 1, 1).astype(LOW)


def first_back_kernel(
    rows_ref, own_ref, other_ref, d_middle_ref, norm_ref, shuffle_ref, d_rows_ref, sums_ref
):
    cut = own_ref.shape[1] // 2
    _, unit, inverse = normalize(rows_ref[...].astype(FULL), norm_ref[0:1, :], norm_ref[2:3, :])
    other = jnp.concatenate([other_ref[:, cut:], other_ref[:, :cut]], axis=1)
    d_normed = own_ref[...] + other.astype(FULL)
    d_rows = d_middle_ref[...] + norm_back(d_normed, unit, inverse, norm_ref[0:1, :])
    d_rows_ref[...] = contract(d_rows.astype(LOW), shuffle_ref[...], 1, 1).astype(LOW)
    sums_ref[0:1, :] = add_up(d_normed * unit)
    sums_ref[1:2, :] = add_up(d_normed)


def build(fsdp, tp):
    bits = fsdp.bit_length() - 1
    masks = sorted(range(fsdp), key=lambda mask: (mask & 1, mask >> 1))

    def flip(array, bit):
        return lax.ppermute(array, "fsdp", [(at, at ^ (1 << bit)) for at in range(fsdp)])

    def flip_tp(array, bit):
        return lax.ppermute(array, "tp", [(at, at ^ (1 << bit)) for at in range(tp)])

    def ahead(array):
        return lax.ppermute(array, "tp", [(at, (at + 1) % tp) for at in range(tp)])

    def trade_rows(array):
        pairs = []
        for row in range(fsdp):
            for column in range(tp):
                odd = (row ^ column) & 1
                pairs.append((row * tp + column, (row ^ odd) * tp + (column ^ odd)))
        return lax.ppermute(array, ("fsdp", "tp"), pairs)

    def sum_everywhere(array):
        for bit in range(bits):
            array = array + flip(array, bit)
        for bit in range(tp.bit_length() - 1):
            array = array + flip_tp(array, bit)
        return array

    def order_of(slot):
        upper = list(range(1, bits))
        return upper if slot % 2 == 0 else upper[::-1]

    def gather_rows(shards, turn):
        rows = shards[0].shape[0]
        count = len(shards)
        order = order_of(turn)
        current = join(shards) if count > 1 else shards[0]
        held = [(0, at) for at in range(count)]
        for bit in order[:-1]:
            both = held + [(mask ^ (1 << bit), at) for mask, at in held]
            arrived = flip(current, bit)
            current, held = join([current, arrived]), both
        last = order[-1]
        arrived = flip(current, last)
        found = [(current, held), (arrived, [(mask ^ (1 << last), at) for mask, at in held])]
        if rows % 16:
            wanted = sorted(found[0][1] + found[1][1], key=lambda item: (item[1], item[0]))
            cut = {}
            for array, items in found:
                for spot, item in enumerate(items):
                    cut[item] = array[spot * rows : (spot + 1) * rows]
            found = [(jnp.concatenate([cut[item] for item in wanted], axis=0), wanted)]
        found += [(flip(array, 0), [(mask ^ 1, at) for mask, at in items]) for array, items in found]
        arrays = [array for array, _ in found]
        sources = []
        for at in range(count):
            pieces = []
            for index, (_, items) in enumerate(found):
                for spot, (mask, shard) in enumerate(items):
                    if shard != at:
                        continue
                    start, put = spot * rows, masks.index(mask) * rows
                    if pieces:
                        source, before, place, length = pieces[-1]
                        if (source, before + length, place + length) == (index, start, put):
                            pieces[-1] = (source, before, place, length + rows)
                            continue
                    pieces.append((index, start, put, rows))
            sources.append((arrays, pieces))
        return sources

    def scatter_rows(kept, sent, turn):
        arrived = flip(sent, 0)
        current = kept.astype(FULL) + arrived.astype(FULL)
        held = [mask for mask in masks if not mask & 1]
        rows = current.shape[-2] // len(held)
        for bit in order_of(turn)[::-1]:
            stay = [at for at, mask in enumerate(held) if not mask >> bit & 1]
            leave = [at for at, mask in enumerate(held) if mask >> bit & 1]

            def pick(positions):
                if positions == list(range(positions[0], positions[0] + len(positions))):
                    return current[..., positions[0] * rows : (positions[-1] + 1) * rows, :]
                return jnp.concatenate(
                    [current[..., at * rows : (at + 1) * rows, :] for at in positions], axis=-2
                )

            arrived = flip(pick(leave).astype(LOW), bit)
            current = pick(stay) + arrived.astype(FULL)
            held = [held[at] for at in stay]
        return current

    def ring(shard):
        slots = [shard]
        for _ in range(1, tp):
            slots.append(ahead(slots[-1]))
        return slots

    def local(
        frames, segments, w_qkv, w_out, w_up, w_down, head_bias, up_bias, ln_gains, shifts, cotangent
    ):
        row = lax.axis_index("fsdp")
        column = lax.axis_index("tp")
        rows, model = frames.shape
        block = model // fsdp
        width = w_qkv.shape[2]
        heads = width // HEAD_DIM
        units = w_up.shape[1]
        fine = ln_gains.shape[1]

        parts = [w_qkv[:, 1], w_qkv[:, 2], w_out.T, w_qkv[:, 0]]
        first_ring = ring(jnp.concatenate(parts, axis=1))
        first_slots = []
        for slot in range(0, tp, 2):
            first_slots += gather_rows(first_ring[slot : slot + 2], slot // 2)
        second_ring = ring(jnp.concatenate([w_up, w_down.T], axis=1))
        second_slots = []
        for slot in range(tp):
            second_slots += gather_rows([second_ring[slot]], slot)

        row_labels = lax.dynamic_index_in_dim(
            segments.reshape(tp, rows), column, 0, keepdims=False
        )
        small = jnp.concatenate(
            [
                ln_gains.reshape(1, -1),
                shifts.reshape(1, -1),
                head_bias.reshape(1, -1),
                up_bias.reshape(1, -1),
                row_labels.astype(LOW)[None],
            ],
            axis=1,
        )
        place = lax.broadcasted_iota(jnp.int32, (fsdp * tp, 1), 0) == row * tp + column
        small = sum_everywhere(jnp.where(place, small, jnp.zeros((), LOW)))
        cut = 6 * fine
        norm_rows = small[:, :cut].reshape(fsdp * tp, 6, fine).transpose(1, 0, 2).reshape(6, model)
        piece = head_bias.shape[1]
        head_rows = small[:, cut : cut + 2 * piece].reshape(fsdp, tp, 2, piece)
        head_rows = head_rows.transpose(1, 2, 0, 3).reshape(tp, 2, width).astype(FULL)
        up_rows = small[:, cut + 2 * piece : -rows].reshape(fsdp, tp, up_bias.shape[0])
        up_rows = up_rows.transpose(1, 0, 2).reshape(tp, 1, units).astype(FULL)

        out_at = lax.broadcasted_iota(jnp.int32, (model, model), 1)
        in_at = lax.broadcasted_iota(jnp.int32, (model, model), 0)
        spot = out_at // block
        mask_at = ((spot & (fsdp // 2 - 1)) << 1) | (spot >> (bits - 1))
        shuffle = (in_at == (row ^ mask_at) * block + out_at % block).astype(LOW)

        norm_rows = contract(norm_rows, shuffle, 1, 0)
        first_row = ((row & -2) | (column & 1)) * tp + (column & -2)

        def labels_of(half):
            found = lax.dynamic_index_in_dim(small, first_row + half, 0, keepdims=False)
            return found[-rows:].astype(jnp.int32)

        own_labels, other_labels = labels_of(row & 1), labels_of(1 - (row & 1))
        all_labels = jnp.concatenate([own_labels, other_labels])

        def extension(labels_part, lead, marks):
            lane = lane_of(labels_part.shape[0])
            clip = lane - (HEAD_DIM + 3)
            values = jnp.where((clip >= 0) & (clip < CLIPS), marks(clip == labels_part[:, None]), 0.0)
            is_lead = (lane >= HEAD_DIM) & (lane < HEAD_DIM + 3)
            return jnp.where(is_lead, lead, values).astype(LOW)

        ext_q = extension(own_labels, 0.0, lambda same: jnp.where(same, 0.0, MASKED))
        ext_k = extension(all_labels, 1.0, lambda same: jnp.where(same, 1.0, 0.0))

        tall = (rows, model)
        wide = (model, rows)
        local_rows, first_low = call_rows(
            first_norm_kernel, ((tall, LOW), (tall, LOW)),
            trade_rows(frames), shuffle, norm_rows,
        )
        first_both, first_t = call_rows(
            both_kernel, (((2 * rows, model), LOW), ((model, 2 * rows), LOW)),
            first_low, flip(first_low, 0),
        )
        seed = trade_rows(cotangent)
        upstream_low, upstream_t = call_rows(
            enter_kernel, ((tall, LOW), (wide, LOW)), seed, shuffle
        )

        def slot_row(array, slot):
            return lax.dynamic_index_in_dim(array, (column - slot + tp) % tp, 0, keepdims=False)

        saved = []
        attended = jnp.zeros((rows, model), FULL)
        none = jnp.zeros((width,), FULL)
        for slot in range(tp):
            bias = slot_row(head_rows, slot)
            bias = jnp.concatenate([none, bias[1], none, bias[0]])[None]
            attended, *kept = attend(
                first_both, first_slots[slot], bias, ext_q, ext_k, attended, heads
            )
            saved.append(kept)
        middle, second_low, second_t = call_rows(
            second_norm_kernel, ((tall, FULL), (tall, LOW), (wide, LOW)),
            local_rows, attended, norm_rows,
        )

        mlp_out = jnp.zeros((rows, model), FULL)
        d_second = jnp.zeros((rows, model), FULL)
        grad_second, unit_sums, grads = [], [], ()
        for slot in range(tp):
            mlp_out, d_second, *grads, sums = mlp(
                second_low, second_t, upstream_low, upstream_t, second_slots[slot],
                slot_row(up_rows, slot), mlp_out, d_second, grads, slot % 2, 2,
            )
            unit_sums.append(sums[0])
            if slot % 2:
                pair = scatter_rows(*grads, slot // 2)
                grad_second += [pair[0], pair[1]]
                grads = ()
        d_middle, d_middle_low, d_middle_t, result, early_sums = call_rows(
            second_back_kernel,
            ((tall, FULL), (tall, LOW), (wide, LOW), (tall, LOW), ((4, model), FULL)),
            middle, d_second, upstream_low, mlp_out, norm_rows, shuffle,
        )
        result = trade_rows(result)

        def ring_sum(parts):
            total = parts[1]
            for slot in list(range(2, tp)) + [0]:
                arrived = ahead(total.astype(LOW))
                total = parts[slot] + arrived.astype(FULL)
            return total

        grad_first = [None] * tp
        head_sums = [None] * tp
        d_own = jnp.zeros((rows, model), FULL)
        d_other = jnp.zeros((rows, model), FULL)
        for slot in list(range(1, tp)) + [0]:
            d_own, d_other, kept, sent, sums = attend_back(
                d_middle_low, d_middle_t, first_t, first_slots[slot], saved[slot],
                d_own, d_other, heads,
            )
            grad_first[slot] = scatter_rows(kept, sent, slot)
            head_sums[slot] = jnp.stack([sums[0, 3 * width :], sums[0, width : 2 * width]])
        d_rows, late_sums = call_rows(
            first_back_kernel, ((tall, LOW), ((2, model), FULL)),
            local_rows, d_own, flip(d_other.astype(LOW), 0), d_middle, norm_rows, shuffle,
        )
        d_rows = trade_rows(d_rows)

        def by_tp(parts):
            at = lax.broadcasted_iota(jnp.int32, (tp,) + (1,) * parts[0].ndim, 0)
            total = 0.0
            for slot, part in enumerate(parts):
                total = total + jnp.where(at == (column - slot + tp) % tp, part[None], 0.0)
            return total

        sums = jnp.concatenate(
            [late_sums[:1], early_sums[:1], late_sums[1:], early_sums[1:]], axis=0
        )
        sums = lax.dot_general(
            sums,
            shuffle.astype(FULL),
            (((1,), (1,)), ((), ())),
            precision=lax.Precision.HIGHEST,
            preferred_element_type=FULL,
        )
        head_part = by_tp(head_sums).transpose(1, 0, 2).reshape(2, tp * width)
        packed = jnp.concatenate([sums, head_part, by_tp(unit_sums).reshape(-1, model)], axis=0)
        packed = sum_everywhere(packed)
        spot_model = (row * tp + column) * fine
        spot_units = column * fsdp + row
        norm_grads = lax.dynamic_slice_in_dim(packed[:6], spot_model, fine, 1)
        gain_grads, shift_grads = norm_grads[:2], norm_grads[2:]
        grad_headbias = lax.dynamic_slice_in_dim(packed[6:8], spot_units * piece, piece, 1)
        grad_upbias = lax.dynamic_slice_in_dim(
            packed[8:].reshape(-1), spot_units * up_bias.shape[0], up_bias.shape[0], 0
        )

        total_first = ring_sum(grad_first)
        total_second = ring_sum(grad_second)
        total_qkv = [total_first[:, at * width : (at + 1) * width] for at in (3, 0, 1)]
        return (
            result,
            d_rows,
            jnp.stack(total_qkv, axis=1),
            total_first[:, 2 * width : 3 * width].T,
            total_second[:, :units],
            total_second[:, units:].T,
            grad_headbias,
            grad_upbias,
            gain_grads,
            shift_grads,
        )

    return local


def solution(mesh):
    placed = (
        P(("fsdp", "tp"), None),
        P("fsdp", None),
        P("fsdp", None, "tp"),
        P("tp", "fsdp"),
        P("fsdp", "tp"),
        P("tp", "fsdp"),
        P(None, ("tp", "fsdp")),
        P(("tp", "fsdp")),
        P(None, ("fsdp", "tp")),
        P(None, ("fsdp", "tp")),
        P(("fsdp", "tp"), None),
    )
    body = build(mesh.shape["fsdp"], mesh.shape["tp"])

    return jax.shard_map(
        body,
        mesh=mesh,
        in_specs=placed,
        out_specs=(
            P(("fsdp", "tp"), None),
            P(("fsdp", "tp"), None),
            P("fsdp", None, "tp"),
            P("tp", "fsdp"),
            P("fsdp", "tp"),
            P("tp", "fsdp"),
            P(None, ("tp", "fsdp")),
            P(("tp", "fsdp")),
            P(None, ("fsdp", "tp")),
            P(None, ("fsdp", "tp")),
        ),
        check_vma=False,
    )
```

```python
import jax
import jax.numpy as jnp
from jax import lax
from jax.experimental import pallas as pl
from jax.experimental.pallas import tpu as pltpu
from jax.sharding import PartitionSpec as P


HEAD_DIM = 64
LANES = 128
CLIPS = 3
EPSILON = 1e-05
MASKED = -1000000000.0
LOW = jnp.bfloat16
FULL = jnp.float32


def normalize(values, gain_row, shift_row):
    average = jnp.mean(values, axis=-1, keepdims=True)
    centered = values - average
    inverse = lax.rsqrt(jnp.mean(centered * centered, axis=-1, keepdims=True) + EPSILON)
    normed = centered * inverse
    return (normed * gain_row + shift_row, normed, inverse)


def norm_back(incoming, normed, inverse, gain_row):
    scaled = incoming * gain_row
    return inverse * (
        scaled
        - jnp.mean(scaled, axis=-1, keepdims=True)
        - normed * jnp.mean(scaled * normed, axis=-1, keepdims=True)
    )


def contract(left, right, left_dim, right_dim):
    return lax.dot_general(
        left, right, (((left_dim,), (right_dim,)), ((), ())), preferred_element_type=FULL
    )


def pieces_of(column):
    high = column.astype(LOW)
    rest = column - high.astype(FULL)
    middle = rest.astype(LOW)
    low = (rest - middle.astype(FULL)).astype(LOW)
    return high, middle, low


def lane_of(rows):
    return lax.broadcasted_iota(jnp.int32, (rows, LANES), 1)


def spread(ref_value, start):
    half = ref_value[:, start : start + HEAD_DIM]
    return jnp.concatenate([half, half], axis=1)


def put_pieces(lane, base, pieces, rest):
    for step, piece in enumerate(pieces):
        rest = jnp.where(lane == base + step, piece, rest)
    return rest


def total_of(terms):
    total = terms[0].astype(FULL)
    for term in terms[1:]:
        total = total + term.astype(FULL)
    return total


ANYWHERE = pl.BlockSpec(memory_space=pltpu.HBM)
WHOLE = pl.BlockSpec(memory_space=pltpu.VMEM)


def outside(arrays):
    return [pltpu.with_memory_space_constraint(array, pltpu.HBM) for array in arrays]


def run_copies(moves, semaphores):
    copies = [
        pltpu.make_async_copy(source, target, semaphores.at[at])
        for at, (source, target) in enumerate(moves)
    ]
    for copy in copies:
        copy.start()
    for copy in copies:
        copy.wait()


def fetch(pieces, refs, target, semaphores):
    run_copies(
        [
            (refs[source].at[pl.ds(start, count)], target.at[pl.ds(put, count)])
            for source, start, put, count in pieces
        ],
        semaphores,
    )


def join(arrays):
    rows, columns = arrays[0].shape
    if rows % 16:
        return jnp.concatenate(arrays, axis=0)
    count = len(arrays)

    def kernel(*refs):
        for at in range(count):
            refs[count][at * rows : (at + 1) * rows, :] = refs[at][...]

    return pl.pallas_call(
        kernel,
        out_shape=jax.ShapeDtypeStruct((count * rows, columns), arrays[0].dtype),
        cost_estimate=pl.CostEstimate(
            flops=0, transcendentals=0, bytes_accessed=4 * count * rows * columns
        ),
        name="join",
    )(*arrays)


def attend_kernel(
    heads, rows, keys, pieces, started, normed_ref, bias_ref, ext_q_ref, ext_k_ref, *refs
):
    if started:
        acc_ref, *refs = refs
    out_ref, mixed_out, q_out, k_out, v_out = refs[-12:-7]
    weight, mixed_ref, q_ref, k_ref, v_ref, semaphores, leaving = refs[-7:]
    width = heads * HEAD_DIM
    fetch(pieces, refs, weight, semaphores)
    lane_q = lane_of(rows)
    lane_k = lane_of(keys)
    ext_k = ext_k_ref[...]
    pair = contract(normed_ref[...], weight[:, : 2 * width], 1, 0) + bias_ref[:, : 2 * width]
    pair = pair.astype(LOW)
    query = contract(normed_ref[:rows, :], weight[:, 2 * width :], 1, 0) + bias_ref[:, 2 * width :]
    query = (query.astype(LOW).astype(FULL) * HEAD_DIM**-0.5).astype(LOW)
    for head in range(heads):
        at = head * HEAD_DIM
        q_ref[head] = jnp.where(lane_q < HEAD_DIM, spread(query, width + at), ext_q_ref[...])
        k_ref[head] = jnp.where(lane_k < HEAD_DIM, spread(pair, at), ext_k)
        v_ref[head] = jnp.where(lane_k < HEAD_DIM, spread(pair, width + at), ext_k)
    saves = [
        pltpu.make_async_copy(source, target, leaving.at[at])
        for at, (source, target) in enumerate(
            ((k_ref, k_out), (v_ref, v_out), (q_ref, q_out), (mixed_ref, mixed_out))
        )
    ]
    saves[0].start()
    saves[1].start()
    for head in range(heads):
        scores = contract(q_ref[head], k_ref[head], 1, 1)
        highest = jnp.max(scores, axis=1, keepdims=True)
        weights = jnp.exp(scores - highest)
        total = jnp.sum(weights, axis=1, keepdims=True)
        mixed = contract(weights.astype(LOW), v_ref[head], 1, 0) / total
        mixed_ref[:, head * HEAD_DIM : (head + 1) * HEAD_DIM] = mixed[:, :HEAD_DIM].astype(LOW)
        pieces = pieces_of(-(highest + jnp.log(total)))
        q_ref[head] = put_pieces(lane_q, HEAD_DIM, pieces, q_ref[head])
    saves[2].start()
    saves[3].start()
    answer = contract(mixed_ref[...], weight[:, 2 * width : 3 * width], 1, 1)
    out_ref[...] = acc_ref[...] + answer if started else answer
    for save in saves:
        save.wait()


def attend(normed, source, bias, ext_q, ext_k, acc, heads):
    arrays, pieces = source
    rows, keys = ext_q.shape[0], ext_k.shape[0]
    model = normed.shape[1]
    saved = [
        ((rows, heads * HEAD_DIM), LOW),
        ((heads, rows, LANES), LOW),
        ((heads, keys, LANES), LOW),
        ((heads, keys, LANES), LOW),
    ]

    def kernel(*refs):
        attend_kernel(heads, rows, keys, pieces, acc is not None, *refs)

    start = [] if acc is None else [acc]
    return pl.pallas_call(
        kernel,
        out_shape=(
            jax.ShapeDtypeStruct((rows, model), FULL),
            *(pltpu.HBM(*item) for item in saved),
        ),
        in_specs=[WHOLE] * (4 + len(start)) + [ANYWHERE] * len(arrays),
        out_specs=(WHOLE,) + (ANYWHERE,) * 4,
        input_output_aliases={4: 0} if start else {},
        scratch_shapes=[
            pltpu.VMEM((model, arrays[0].shape[1]), LOW),
            *(pltpu.VMEM(*item) for item in saved),
            pltpu.SemaphoreType.DMA((len(pieces),)),
            pltpu.SemaphoreType.DMA((4,)),
        ],
        cost_estimate=pl.CostEstimate(
            flops=4 * heads * rows * keys * LANES + 8 * rows * model * heads * HEAD_DIM,
            transcendentals=heads * rows * keys,
            bytes_accessed=2 * (normed.size + 4 * rows * model + 8 * rows * heads * LANES),
        ),
        compiler_params=pltpu.CompilerParams(vmem_limit_bytes=26 << 20),
        name="attend",
    )(normed, bias, ext_q, ext_k, *start, *outside(arrays))


def mlp_kernel(
    block, pieces, place, started,
    normed_ref, normed_t_ref, seed_ref, seed_t_ref, bias_ref, *refs
):
    if started:
        out_in_ref, d_in_ref, *refs = refs
    out_ref, d_ref, kept_out, sent_out, sums_ref = refs[-10:-5]
    weight, kept_ref, sent_ref, semaphores, leaving = refs[-5:]
    cut = kept_ref.shape[0]
    units = bias_ref.shape[1]

    def spans(at):
        return (
            pl.ds(pl.multiple_of(at * block, block), block),
            pl.ds(pl.multiple_of(units + at * block, block), block),
        )

    def copies(at):
        return [
            pltpu.make_async_copy(
                refs[source].at[pl.ds(start, count), span],
                weight.at[pl.ds(put, count), span],
                semaphores.at[at, 2 * order + side],
            )
            for order, (source, start, put, count) in enumerate(pieces)
            for side, span in enumerate(spans(at))
        ]

    def saves(at):
        return [
            pltpu.make_async_copy(
                source.at[:, span], target.at[place, :, span], leaving.at[at, 2 * order + side]
            )
            for order, (source, target) in enumerate(((kept_ref, kept_out), (sent_ref, sent_out)))
            for side, span in enumerate(spans(at))
        ]

    for at in range(units // block):
        for copy in copies(at):
            copy.start()
    out_ref[...] = out_in_ref[...] if started else jnp.zeros(out_ref.shape, FULL)
    d_ref[...] = d_in_ref[...] if started else jnp.zeros(d_ref.shape, FULL)

    def step(at, carry):
        span_up, span_down = spans(at)
        for copy in copies(at):
            copy.wait()
        up = contract(normed_ref[...], weight[:, span_up], 1, 0) + bias_ref[:, span_up]
        d_active = contract(seed_ref[...], weight[:, span_down], 1, 0)
        cumulative = 0.5 + 0.5 * lax.erf(up * 0.7071067811865476)
        active = (up * cumulative).astype(LOW)
        slope = cumulative + up * (jnp.exp(-0.5 * up * up) * 0.3989422804014327)
        d_up = (d_active * slope).astype(LOW)
        sums_ref[:, span_up] = jnp.sum(d_up.astype(FULL), axis=0, keepdims=True)
        out_ref[...] += contract(active, weight[:, span_down], 1, 1)
        d_ref[...] += contract(d_up, weight[:, span_up], 1, 1)
        grad_up = contract(normed_t_ref[...], d_up, 1, 0).astype(LOW)
        kept_ref[:, span_up] = grad_up[:cut]
        sent_ref[:, span_up] = grad_up[cut:]
        grad_down = contract(seed_t_ref[...], active, 1, 0).astype(LOW)
        kept_ref[:, span_down] = grad_down[:cut]
        sent_ref[:, span_down] = grad_down[cut:]
        for save in saves(at):
            save.start()
        return carry

    lax.fori_loop(0, units // block, step, 0)
    for at in range(units // block):
        for save in saves(at):
            save.wait()


def mlp(normed, normed_t, seed, seed_t, source, bias, out, d_normed, grads, at, total):
    arrays, pieces = source
    rows, model = normed.shape
    units = bias.shape[1]
    cut = model // 2

    def kernel(*refs):
        mlp_kernel(256, pieces, at, out is not None, *refs)

    grad_shape = pltpu.HBM((total, cut, 2 * units), LOW)
    grads = list(grads)
    start = [] if out is None else [out, d_normed]
    first = 5 + len(start) + len(arrays)
    return pl.pallas_call(
        kernel,
        out_shape=(
            jax.ShapeDtypeStruct((rows, model), FULL),
            jax.ShapeDtypeStruct((rows, model), FULL),
            grad_shape,
            grad_shape,
            jax.ShapeDtypeStruct((1, units), FULL),
        ),
        in_specs=[WHOLE] * (5 + len(start)) + [ANYWHERE] * (len(arrays) + len(grads)),
        out_specs=(WHOLE, WHOLE, ANYWHERE, ANYWHERE, WHOLE),
        input_output_aliases={
            **({5: 0, 6: 1} if start else {}),
            **({first: 2, first + 1: 3} if grads else {}),
        },
        scratch_shapes=[
            pltpu.VMEM((model, 2 * units), LOW),
            pltpu.VMEM((cut, 2 * units), LOW),
            pltpu.VMEM((cut, 2 * units), LOW),
            pltpu.SemaphoreType.DMA((units // 256, 2 * len(pieces))),
            pltpu.SemaphoreType.DMA((units // 256, 4)),
        ],
        cost_estimate=pl.CostEstimate(
            flops=12 * rows * model * units,
            transcendentals=2 * rows * units,
            bytes_accessed=16 * rows * model + 8 * model * units,
        ),
        compiler_params=pltpu.CompilerParams(vmem_limit_bytes=26 << 20),
        name="mlp",
    )(normed, normed_t, seed, seed_t, bias, *start, *outside(arrays), *outside(grads))


def back_kernel(
    heads, rows, keys, pieces, started, d_ref, d_t_ref, normed_t_ref, *refs
):
    if started:
        own_in_ref, other_in_ref, *refs = refs
    q_in, k_in, v_in, mixed_in, *refs = refs
    own_ref, other_ref, kept_out, sent_out, sums_ref = refs[-19:-14]
    (
        weight, q_ref, k_ref, v_ref, mixed_ref, kept_ref, sent_ref,
        u_buf, dq_buf, dk_buf, dv_buf, pair_buf, query_buf, semaphores,
    ) = refs[-14:]
    width = heads * HEAD_DIM
    cut = kept_ref.shape[0]
    first = len(pieces)
    entering = [
        pltpu.make_async_copy(source, target, semaphores.at[first + at])
        for at, (source, target) in enumerate(
            ((mixed_in, mixed_ref), (q_in, q_ref), (k_in, k_ref), (v_in, v_ref))
        )
    ]
    for copy in entering:
        copy.start()
    fetch(pieces, refs, weight, semaphores)
    lane_q = lane_of(rows)
    upstream_all = contract(d_ref[...], weight[:, 2 * width : 3 * width], 1, 0).astype(LOW)
    entering[0].wait()
    mixed = mixed_ref[...]
    for head in range(heads):
        at = head * HEAD_DIM
        product = upstream_all[:, at : at + HEAD_DIM].astype(FULL) * mixed[
            :, at : at + HEAD_DIM
        ].astype(FULL)
        pieces_here = pieces_of(-jnp.sum(product, axis=1, keepdims=True))
        rest = jnp.where(lane_q < HEAD_DIM, spread(upstream_all, at), jnp.zeros((), LOW))
        u_buf[head] = put_pieces(lane_q, HEAD_DIM, pieces_here, rest)
    for copy in entering[1:]:
        copy.wait()
    block = 256

    def one_head(head, carry):
        queries = q_ref[head]
        upstream = u_buf[head]
        total = jnp.zeros((rows, LANES), FULL)
        for start in range(0, keys, block):
            span = pl.ds(start, block)
            keys_part = k_ref[head, span, :]
            shares = jnp.exp(contract(keys_part, queries, 1, 1))
            d_scores = (shares * contract(v_ref[head, span, :], upstream, 1, 1)).astype(LOW)
            dv_buf[head, span, :] = contract(shares.astype(LOW), upstream, 1, 0).astype(LOW)
            dk_buf[head, span, :] = contract(d_scores, queries, 1, 0).astype(LOW)
            total = total + contract(d_scores, keys_part, 0, 0)
        dq_buf[head] = (total * HEAD_DIM**-0.5).astype(LOW)
        return carry

    lax.fori_loop(0, heads, one_head, 0)
    query_buf[:, :width] = jnp.zeros((rows, width), LOW)
    for head in range(heads):
        at = head * HEAD_DIM
        query_buf[:, width + at : width + at + HEAD_DIM] = dq_buf[head][:, :HEAD_DIM]
        pair_buf[:, at : at + HEAD_DIM] = dk_buf[head][:, :HEAD_DIM]
        pair_buf[:, width + at : width + at + HEAD_DIM] = dv_buf[head][:, :HEAD_DIM]
    grad_pair = contract(normed_t_ref[...], pair_buf[...], 1, 0).astype(LOW)
    kept_ref[:, : 2 * width] = grad_pair[:cut]
    sent_ref[:, : 2 * width] = grad_pair[cut:]
    grad_query = contract(normed_t_ref[:, :rows], query_buf[...], 1, 0).astype(LOW)
    kept_ref[:, 2 * width :] = grad_query[:cut]
    sent_ref[:, 2 * width :] = grad_query[cut:]
    grad_out = contract(d_t_ref[...], mixed, 1, 0).astype(LOW)
    kept_ref[:, 2 * width : 3 * width] = grad_out[:cut]
    sent_ref[:, 2 * width : 3 * width] = grad_out[cut:]
    saves = [
        pltpu.make_async_copy(kept_ref, kept_out, semaphores.at[first + 4]),
        pltpu.make_async_copy(sent_ref, sent_out, semaphores.at[first + 5]),
    ]
    for save in saves:
        save.start()
    sums_ref[:, : 2 * width] = jnp.sum(pair_buf[...].astype(FULL), axis=0, keepdims=True)
    sums_ref[:, 2 * width :] = jnp.sum(query_buf[...].astype(FULL), axis=0, keepdims=True)
    own = contract(pair_buf[:rows, :], weight[:, : 2 * width], 1, 1) + contract(
        query_buf[...], weight[:, 2 * width :], 1, 1
    )
    own_ref[...] = own_in_ref[...] + own if started else own
    other = contract(pair_buf[rows:, :], weight[:, : 2 * width], 1, 1)
    other_ref[...] = (other_in_ref[...] + other if started else other).astype(other_ref.dtype)
    for save in saves:
        save.wait()


def attend_back(d_middle, d_middle_t, normed_t, source, saved, own, other, heads, last):
    arrays, pieces = source
    mixed, queries, keys_all, values = saved
    rows, keys = d_middle.shape[0], normed_t.shape[1]
    model = normed_t.shape[0]
    cut, columns = model // 2, arrays[0].shape[1]
    width = heads * HEAD_DIM

    def kernel(*refs):
        back_kernel(heads, rows, keys, pieces, own is not None, *refs)

    start = [] if own is None else [own, other]
    aliases = {3: 0, 4: 1} if start else {}
    if last:
        aliases.pop(4)
    return pl.pallas_call(
        kernel,
        out_shape=(
            jax.ShapeDtypeStruct((rows, model), FULL),
            jax.ShapeDtypeStruct((rows, model), LOW if last else FULL),
            pltpu.HBM((cut, columns), LOW),
            pltpu.HBM((cut, columns), LOW),
            jax.ShapeDtypeStruct((1, columns), FULL),
        ),
        in_specs=[WHOLE] * (3 + len(start)) + [ANYWHERE] * (4 + len(arrays)),
        out_specs=(WHOLE, WHOLE, ANYWHERE, ANYWHERE, WHOLE),
        input_output_aliases=aliases,
        scratch_shapes=[
            pltpu.VMEM((model, columns), LOW),
            pltpu.VMEM((heads, rows, LANES), LOW),
            pltpu.VMEM((heads, keys, LANES), LOW),
            pltpu.VMEM((heads, keys, LANES), LOW),
            pltpu.VMEM((rows, width), LOW),
            pltpu.VMEM((cut, columns), LOW),
            pltpu.VMEM((cut, columns), LOW),
            pltpu.VMEM((heads, rows, LANES), LOW),
            pltpu.VMEM((heads, rows, LANES), LOW),
            pltpu.VMEM((heads, keys, LANES), LOW),
            pltpu.VMEM((heads, keys, LANES), LOW),
            pltpu.VMEM((keys, 2 * width), LOW),
            pltpu.VMEM((rows, columns - 2 * width), LOW),
            pltpu.SemaphoreType.DMA((len(pieces) + 6,)),
        ],
        cost_estimate=pl.CostEstimate(
            flops=10 * heads * rows * keys * LANES + 20 * rows * model * width,
            transcendentals=heads * rows * keys,
            bytes_accessed=8 * keys * model + 8 * rows * model,
        ),
        compiler_params=pltpu.CompilerParams(vmem_limit_bytes=28 << 20),
        name="attend_back",
    )(
        d_middle, d_middle_t, normed_t, *start,
        *outside((queries, keys_all, values, mixed)), *outside(arrays),
    )


def call_rows(kernel, shapes, *arrays):
    return pl.pallas_call(
        kernel,
        out_shape=tuple(jax.ShapeDtypeStruct(*shape) for shape in shapes),
        in_specs=[WHOLE] * len(arrays),
        out_specs=(WHOLE,) * len(shapes),
        cost_estimate=pl.CostEstimate(
            flops=2 * arrays[0].size * arrays[0].shape[1],
            transcendentals=0,
            bytes_accessed=sum(array.size * array.dtype.itemsize for array in arrays),
        ),
        compiler_params=pltpu.CompilerParams(vmem_limit_bytes=24 << 20),
    )(*arrays)


def pack_kernel(
    rows, spots_ref, gains_ref, shifts_ref, heads_ref, ups_ref, labels_ref, out_ref, line
):
    at = 0
    for ref in (gains_ref, shifts_ref, heads_ref, ups_ref):
        count, size = ref.shape
        for which in range(count):
            line[:, at : at + size] = ref[which : which + 1, :].astype(FULL)
            at += size
    start = pl.multiple_of(spots_ref[2], LANES)
    line[:, at:] = labels_ref[pl.ds(spots_ref[1], 1), pl.ds(start, rows)].astype(FULL)
    place = lax.broadcasted_iota(jnp.int32, out_ref.shape, 0) == spots_ref[0]
    out_ref[...] = jnp.where(place, jnp.broadcast_to(line[...], out_ref.shape), 0.0).astype(LOW)


def pack_small(spots, devices, rows, *arrays):
    size = sum(array.size for array in arrays[:-1]) + rows

    def kernel(*refs):
        pack_kernel(rows, *refs)

    return pl.pallas_call(
        kernel,
        out_shape=jax.ShapeDtypeStruct((devices, size), LOW),
        in_specs=[pl.BlockSpec(memory_space=pltpu.SMEM)] + [WHOLE] * len(arrays),
        out_specs=WHOLE,
        scratch_shapes=[pltpu.VMEM((1, size), FULL)],
        name="pack_small",
    )(spots, *arrays)


def pick_kernel(starts_ref, sums_ref, gains_ref, shifts_ref, heads_ref, ups_ref):
    total = sums_ref.shape[1]

    def window(first, count, which, size):
        moved = pltpu.roll(sums_ref[...], (total - starts_ref[which]) % total, 1)
        return moved[first : first + count, :size]

    fine, piece, unit = gains_ref.shape[1], heads_ref.shape[1], ups_ref.shape[1]
    gains_ref[...] = window(0, 2, 0, fine)
    shifts_ref[...] = window(2, 4, 0, fine)
    heads_ref[0:1, :] = window(6, 1, 2, piece)
    heads_ref[1:2, :] = window(6, 1, 1, piece)
    ups_ref[...] = window(7, 1, 3, unit)


def pick_own(starts, sums, fine, piece, unit):
    return pl.pallas_call(
        pick_kernel,
        out_shape=tuple(
            jax.ShapeDtypeStruct(shape, FULL)
            for shape in ((2, fine), (4, fine), (2, piece), (1, unit))
        ),
        in_specs=[pl.BlockSpec(memory_space=pltpu.SMEM), WHOLE],
        name="pick_own",
    )(starts, sums)


def enter_kernel(rows_ref, shuffle_ref, out_ref, out_t_ref):
    moved = contract(rows_ref[...], shuffle_ref[...], 1, 0).astype(LOW)
    out_ref[...] = moved
    out_t_ref[...] = moved.T


def first_norm_kernel(rows_ref, shuffle_ref, norm_ref, rows_out, normed_ref):
    moved = contract(rows_ref[...], shuffle_ref[...], 1, 0)
    rows_out[...] = moved.astype(LOW)
    normed_ref[...] = normalize(moved, norm_ref[0:1, :], norm_ref[2:3, :])[0].astype(LOW)


def both_kernel(own_ref, other_ref, both_ref, both_t_ref):
    rows, model = own_ref.shape
    cut = model // 2
    both_ref[:rows, :] = own_ref[...]
    both_ref[rows:, :cut] = other_ref[:, cut:]
    both_ref[rows:, cut:] = other_ref[:, :cut]
    both_t_ref[...] = both_ref[...].T


def second_norm_kernel(rows_ref, attended_ref, norm_ref, middle_ref, normed_ref, normed_t_ref):
    middle = rows_ref[...].astype(FULL) + attended_ref[...] + norm_ref[4:5, :]
    middle_ref[...] = middle
    normed = normalize(middle, norm_ref[1:2, :], norm_ref[3:4, :])[0].astype(LOW)
    normed_ref[...] = normed
    normed_t_ref[...] = normed.T


def add_up(array):
    return jnp.sum(array, axis=0, keepdims=True)


def second_back_kernel(
    middle_ref, d_normed_ref, seed_ref, mlp_ref, norm_ref, shuffle_ref,
    d_ref, d_low_ref, d_t_ref, result_ref, sums_ref,
):
    middle = middle_ref[...]
    _, unit, inverse = normalize(middle, norm_ref[1:2, :], norm_ref[3:4, :])
    d_normed = d_normed_ref[...]
    seed = seed_ref[...].astype(FULL)
    d_middle = seed + norm_back(d_normed, unit, inverse, norm_ref[1:2, :])
    d_ref[...] = d_middle
    low = d_middle.astype(LOW)
    d_low_ref[...] = low
    d_t_ref[...] = low.T
    sums_ref[0:1, :] = add_up(d_normed * unit)
    sums_ref[1:2, :] = add_up(d_normed)
    sums_ref[2:3, :] = add_up(d_middle)
    sums_ref[3:4, :] = add_up(seed)
    result = (middle + mlp_ref[...] + norm_ref[5:6, :]).astype(LOW)
    result_ref[...] = contract(result, shuffle_ref[...], 1, 1).astype(LOW)


def first_back_kernel(
    rows_ref, own_ref, other_ref, d_middle_ref, norm_ref, shuffle_ref, d_rows_ref, sums_ref
):
    cut = own_ref.shape[1] // 2
    _, unit, inverse = normalize(rows_ref[...].astype(FULL), norm_ref[0:1, :], norm_ref[2:3, :])
    other = jnp.concatenate([other_ref[:, cut:], other_ref[:, :cut]], axis=1)
    d_normed = own_ref[...] + other.astype(FULL)
    d_rows = d_middle_ref[...] + norm_back(d_normed, unit, inverse, norm_ref[0:1, :])
    d_rows_ref[...] = contract(d_rows.astype(LOW), shuffle_ref[...], 1, 1).astype(LOW)
    sums_ref[0:1, :] = add_up(d_normed * unit)
    sums_ref[1:2, :] = add_up(d_normed)


def build(fsdp, tp):
    bits = fsdp.bit_length() - 1
    masks = sorted(range(fsdp), key=lambda mask: (mask & 1, mask >> 1))

    def flip(array, bit):
        return lax.ppermute(array, "fsdp", [(at, at ^ (1 << bit)) for at in range(fsdp)])

    def flip_tp(array, bit):
        return lax.ppermute(array, "tp", [(at, at ^ (1 << bit)) for at in range(tp)])

    def trade_rows(array):
        pairs = []
        for row in range(fsdp):
            for column in range(tp):
                odd = (row ^ column) & 1
                pairs.append((row * tp + column, (row ^ odd) * tp + (column ^ odd)))
        return lax.ppermute(array, ("fsdp", "tp"), pairs)

    def sum_everywhere(array):
        for bit in range(bits):
            array = array + flip(array, bit)
        for bit in range(tp.bit_length() - 1):
            array = array + flip_tp(array, bit)
        return array

    def order_of(slot):
        upper = list(range(1, bits))
        return upper if slot % 2 == 0 else upper[::-1]

    def gather_rows(current, count, turn):
        rows = current.shape[0] // count
        order = order_of(turn)
        held = [(0, at) for at in range(count)]
        for bit in order[:-1]:
            both = held + [(mask ^ (1 << bit), at) for mask, at in held]
            arrived = flip(current, bit)
            current, held = join([current, arrived]), both
        last = order[-1]
        arrived = flip(current, last)
        found = [(current, held), (arrived, [(mask ^ (1 << last), at) for mask, at in held])]
        if rows % 16:
            wanted = sorted(found[0][1] + found[1][1], key=lambda item: (item[1], item[0]))
            cut = {}
            for array, items in found:
                for spot, item in enumerate(items):
                    cut[item] = array[spot * rows : (spot + 1) * rows]
            found = [(jnp.concatenate([cut[item] for item in wanted], axis=0), wanted)]
        found += [(flip(array, 0), [(mask ^ 1, at) for mask, at in items]) for array, items in found]
        arrays = [array for array, _ in found]
        sources = []
        for at in range(count):
            pieces = []
            for index, (_, items) in enumerate(found):
                for spot, (mask, shard) in enumerate(items):
                    if shard != at:
                        continue
                    start, put = spot * rows, masks.index(mask) * rows
                    if pieces:
                        source, before, place, length = pieces[-1]
                        if (source, before + length, place + length) == (index, start, put):
                            pieces[-1] = (source, before, place, length + rows)
                            continue
                    pieces.append((index, start, put, rows))
            sources.append((arrays, pieces))
        return sources

    def scatter_rows(kept, sent, turn):
        arrived = flip(sent, 0)
        terms = [kept, arrived]
        held = [mask for mask in masks if not mask & 1]
        rows = kept.shape[-2] // len(held)

        def pick(array, positions):
            if positions == list(range(positions[0], positions[0] + len(positions))):
                return array[..., positions[0] * rows : (positions[-1] + 1) * rows, :]
            return jnp.concatenate(
                [array[..., at * rows : (at + 1) * rows, :] for at in positions], axis=-2
            )

        for bit in order_of(turn)[::-1]:
            stay = [at for at, mask in enumerate(held) if not mask >> bit & 1]
            leave = [at for at, mask in enumerate(held) if mask >> bit & 1]
            leaving = total_of([pick(term, leave) for term in terms]).astype(LOW)
            arrived = flip(leaving, bit)
            terms = [pick(term, stay) for term in terms] + [arrived]
            held = [held[at] for at in stay]
        return terms

    tp_bits = tp.bit_length() - 1

    def spread_tp(shard):
        slots = [shard]
        for bit in range(tp_bits):
            for at in range(1 << bit):
                slots.append(flip_tp(slots[at], bit))
        return slots

    def local(
        frames, segments, w_qkv, w_out, w_up, w_down, head_bias, up_bias, ln_gains, shifts, cotangent
    ):
        row = lax.axis_index("fsdp")
        column = lax.axis_index("tp")
        rows, model = frames.shape
        block = model // fsdp
        width = w_qkv.shape[2]
        heads = width // HEAD_DIM
        units = w_up.shape[1]
        fine = ln_gains.shape[1]

        parts = [w_qkv[:, 1], w_qkv[:, 2], w_out.T, w_qkv[:, 0]]
        first_shard = jnp.concatenate(parts, axis=1)
        second_shard = jnp.concatenate([w_up, w_down.T], axis=1)
        first_parts = spread_tp(first_shard)
        pairs = [join(first_parts[at : at + 2]) for at in range(0, tp, 2)]
        first_slots = []
        for at, pair in enumerate(pairs):
            first_slots += gather_rows(pair, 2, at)
        second_slots = []
        for slot, shard in enumerate(spread_tp(second_shard)):
            second_slots += gather_rows(shard, 1, 2 * slot // tp)

        here = tp // segments.shape[0]
        spots = jnp.stack([row * tp + column, column // here, column % here * rows])
        small = sum_everywhere(
            pack_small(
                spots, fsdp * tp, rows,
                ln_gains, shifts, head_bias, up_bias.reshape(1, -1), segments,
            )
        )
        cut = 6 * fine
        norm_rows = small[:, :cut].reshape(fsdp * tp, 6, fine).transpose(1, 0, 2).reshape(6, model)
        piece = head_bias.shape[1]
        head_rows = small[:, cut : cut + 2 * piece].reshape(fsdp, tp, 2, piece)
        head_rows = head_rows.transpose(1, 2, 0, 3).reshape(tp, 2, width).astype(FULL)
        up_rows = small[:, cut + 2 * piece : -rows].reshape(fsdp, tp, up_bias.shape[0])
        up_rows = up_rows.transpose(1, 0, 2).reshape(tp, 1, units).astype(FULL)

        out_at = lax.broadcasted_iota(jnp.int32, (model, model), 1)
        in_at = lax.broadcasted_iota(jnp.int32, (model, model), 0)
        spot = out_at // block
        mask_at = ((spot & (fsdp // 2 - 1)) << 1) | (spot >> (bits - 1))
        shuffle = (in_at == (row ^ mask_at) * block + out_at % block).astype(LOW)

        norm_rows = contract(norm_rows, shuffle, 1, 0)
        first_row = ((row & -2) | (column & 1)) * tp + (column & -2)

        def labels_of(half):
            found = lax.dynamic_index_in_dim(small, first_row + half, 0, keepdims=False)
            return found[-rows:].astype(jnp.int32)

        own_labels, other_labels = labels_of(row & 1), labels_of(1 - (row & 1))
        all_labels = jnp.concatenate([own_labels, other_labels])

        def extension(labels_part, lead, marks):
            lane = lane_of(labels_part.shape[0])
            clip = lane - (HEAD_DIM + 3)
            values = jnp.where((clip >= 0) & (clip < CLIPS), marks(clip == labels_part[:, None]), 0.0)
            is_lead = (lane >= HEAD_DIM) & (lane < HEAD_DIM + 3)
            return jnp.where(is_lead, lead, values).astype(LOW)

        ext_q = extension(own_labels, 0.0, lambda same: jnp.where(same, 0.0, MASKED))
        ext_k = extension(all_labels, 1.0, lambda same: jnp.where(same, 1.0, 0.0))

        tall = (rows, model)
        wide = (model, rows)
        local_rows, first_low = call_rows(
            first_norm_kernel, ((tall, LOW), (tall, LOW)),
            trade_rows(frames), shuffle, norm_rows,
        )
        first_both, first_t = call_rows(
            both_kernel, (((2 * rows, model), LOW), ((model, 2 * rows), LOW)),
            first_low, flip(first_low, 0),
        )
        seed = trade_rows(cotangent)
        upstream_low, upstream_t = call_rows(
            enter_kernel, ((tall, LOW), (wide, LOW)), seed, shuffle
        )

        def slot_row(array, slot):
            return lax.dynamic_index_in_dim(array, column ^ slot, 0, keepdims=False)

        saved = []
        attended = None
        none = jnp.zeros((width,), FULL)
        for slot in range(tp):
            bias = slot_row(head_rows, slot)
            bias = jnp.concatenate([none, bias[1], none, bias[0]])[None]
            attended, *kept = attend(
                first_both, first_slots[slot], bias, ext_q, ext_k, attended, heads
            )
            saved.append(kept)
        middle, second_low, second_t = call_rows(
            second_norm_kernel, ((tall, FULL), (tall, LOW), (wide, LOW)),
            local_rows, attended, norm_rows,
        )

        mlp_out = d_second = None
        grad_second, unit_sums, grads = [], [], ()
        for slot in range(tp):
            mlp_out, d_second, *grads, sums = mlp(
                second_low, second_t, upstream_low, upstream_t, second_slots[slot],
                slot_row(up_rows, slot), mlp_out, d_second, grads, slot % 2, 2,
            )
            unit_sums.append(sums)
            if slot % 2:
                grad_second.append(scatter_rows(*grads, slot // 2))
                grads = ()
        d_middle, d_middle_low, d_middle_t, result, early_sums = call_rows(
            second_back_kernel,
            ((tall, FULL), (tall, LOW), (wide, LOW), (tall, LOW), ((4, model), FULL)),
            middle, d_second, upstream_low, mlp_out, norm_rows, shuffle,
        )
        result = trade_rows(result)

        def sum_tp(parts):
            for bit in range(tp_bits):
                for slot in range(tp - (1 << bit), 0, -(2 << bit)):
                    arrived = flip_tp(total_of(parts[slot]).astype(LOW), bit)
                    parts[slot ^ (1 << bit)] = parts[slot ^ (1 << bit)] + [arrived]
            return total_of(parts[0])

        grad_first = [None] * tp
        head_sums = [None] * tp
        d_own = d_other = None
        for slot in range(tp - 1, -1, -1):
            d_own, d_other, kept, sent, sums = attend_back(
                d_middle_low, d_middle_t, first_t, first_slots[slot], saved[slot],
                d_own, d_other, heads, slot == 0,
            )
            grad_first[slot] = scatter_rows(kept, sent, slot)
            head_sums[slot] = sums
        d_rows, late_sums = call_rows(
            first_back_kernel, ((tall, LOW), ((2, model), FULL)),
            local_rows, d_own, flip(d_other, 0), d_middle, norm_rows, shuffle,
        )
        d_rows = trade_rows(d_rows)

        sums = jnp.concatenate(
            [late_sums[:1], early_sums[:1], late_sums[1:], early_sums[1:]], axis=0
        )
        sums = lax.dot_general(
            sums,
            shuffle.astype(FULL),
            (((1,), (1,)), ((), ())),
            precision=lax.Precision.HIGHEST,
            preferred_element_type=FULL,
        )
        packed = jnp.concatenate(
            [sums] + [item for pair in zip(head_sums, unit_sums) for item in pair], axis=0
        )
        for bit in range(tp_bits - 1, -1, -1):
            keep = 6 + 2 * (1 << bit)
            arrived = flip_tp(jnp.concatenate([packed[:6], packed[keep:]], axis=0), bit)
            packed = packed[:keep] + arrived
        for bit in range(bits):
            packed = packed + flip(packed, bit)
        starts = jnp.stack(
            [(row * tp + column) * fine, width + row * piece, 3 * width + row * piece, row * up_bias.shape[0]]
        )
        gain_grads, shift_grads, grad_headbias, grad_upbias = pick_own(
            starts, packed, fine, piece, up_bias.shape[0]
        )
        grad_upbias = grad_upbias[0]

        total_first = sum_tp(grad_first)
        total_second = sum_tp([[term[at % 2] for term in grad_second[at // 2]] for at in range(tp)])
        total_qkv = [total_first[:, at * width : (at + 1) * width] for at in (3, 0, 1)]
        return (
            result,
            d_rows,
            jnp.stack(total_qkv, axis=1),
            total_first[:, 2 * width : 3 * width].T,
            total_second[:, :units],
            total_second[:, units:].T,
            grad_headbias,
            grad_upbias,
            gain_grads,
            shift_grads,
        )

    return local


def solution(mesh):
    placed = (
        P(("fsdp", "tp"), None),
        P("fsdp", None),
        P("fsdp", None, "tp"),
        P("tp", "fsdp"),
        P("fsdp", "tp"),
        P("tp", "fsdp"),
        P(None, ("tp", "fsdp")),
        P(("tp", "fsdp")),
        P(None, ("fsdp", "tp")),
        P(None, ("fsdp", "tp")),
        P(("fsdp", "tp"), None),
    )
    body = build(mesh.shape["fsdp"], mesh.shape["tp"])

    return jax.shard_map(
        body,
        mesh=mesh,
        in_specs=placed,
        out_specs=(
            P(("fsdp", "tp"), None),
            P(("fsdp", "tp"), None),
            P("fsdp", None, "tp"),
            P("tp", "fsdp"),
            P("fsdp", "tp"),
            P("tp", "fsdp"),
            P(None, ("tp", "fsdp")),
            P(("tp", "fsdp")),
            P(None, ("fsdp", "tp")),
            P(None, ("fsdp", "tp")),
        ),
        check_vma=False,
    )
```

```python
import jax
import jax.numpy as jnp
from jax import lax
from jax.experimental import pallas as pl
from jax.experimental.pallas import tpu as pltpu
from jax.sharding import PartitionSpec as P


HEAD_DIM = 64
LANES = 128
CLIPS = 3
EPSILON = 1e-05
MASKED = -1000000000.0
LOW = jnp.bfloat16
FULL = jnp.float32


def normalize(values, gain_row, shift_row):
    average = jnp.mean(values, axis=-1, keepdims=True)
    centered = values - average
    inverse = lax.rsqrt(jnp.mean(centered * centered, axis=-1, keepdims=True) + EPSILON)
    normed = centered * inverse
    return (normed * gain_row + shift_row, normed, inverse)


def norm_back(incoming, normed, inverse, gain_row):
    scaled = incoming * gain_row
    return inverse * (
        scaled
        - jnp.mean(scaled, axis=-1, keepdims=True)
        - normed * jnp.mean(scaled * normed, axis=-1, keepdims=True)
    )


def contract(left, right, left_dim, right_dim):
    return lax.dot_general(
        left, right, (((left_dim,), (right_dim,)), ((), ())), preferred_element_type=FULL
    )


def pieces_of(column):
    high = column.astype(LOW)
    rest = column - high.astype(FULL)
    middle = rest.astype(LOW)
    low = (rest - middle.astype(FULL)).astype(LOW)
    return high, middle, low


def lane_of(rows):
    return lax.broadcasted_iota(jnp.int32, (rows, LANES), 1)


def spread(ref_value, start):
    half = ref_value[:, start : start + HEAD_DIM]
    return jnp.concatenate([half, half], axis=1)


def put_pieces(lane, base, pieces, rest):
    for step, piece in enumerate(pieces):
        rest = jnp.where(lane == base + step, piece, rest)
    return rest


def total_of(terms):
    total = terms[0].astype(FULL)
    for term in terms[1:]:
        total = total + term.astype(FULL)
    return total


ANYWHERE = pl.BlockSpec(memory_space=pltpu.HBM)
WHOLE = pl.BlockSpec(memory_space=pltpu.VMEM)


def outside(arrays):
    return [pltpu.with_memory_space_constraint(array, pltpu.HBM) for array in arrays]


def run_copies(moves, semaphores):
    copies = [
        pltpu.make_async_copy(source, target, semaphores.at[at])
        for at, (source, target) in enumerate(moves)
    ]
    for copy in copies:
        copy.start()
    for copy in copies:
        copy.wait()


def fetch(pieces, refs, target, semaphores):
    run_copies(
        [
            (refs[source].at[pl.ds(start, count)], target.at[pl.ds(put, count)])
            for source, start, put, count in pieces
        ],
        semaphores,
    )


def join(arrays):
    rows, columns = arrays[0].shape
    if rows % 16:
        return jnp.concatenate(arrays, axis=0)
    count = len(arrays)

    def kernel(*refs):
        for at in range(count):
            refs[count][at * rows : (at + 1) * rows, :] = refs[at][...]

    return pl.pallas_call(
        kernel,
        out_shape=jax.ShapeDtypeStruct((count * rows, columns), arrays[0].dtype),
        cost_estimate=pl.CostEstimate(
            flops=0, transcendentals=0, bytes_accessed=4 * count * rows * columns
        ),
        compiler_params=pltpu.CompilerParams(vmem_limit_bytes=6 << 20),
        name="join",
    )(*arrays)


def attend_kernel(
    heads, rows, keys, pieces, started, normed_ref, bias_ref, ext_q_ref, ext_k_ref, *refs
):
    if started:
        acc_ref, *refs = refs
    out_ref, mixed_out, q_out, k_out, v_out = refs[-12:-7]
    weight, mixed_ref, q_ref, k_ref, v_ref, semaphores, leaving = refs[-7:]
    width = heads * HEAD_DIM
    fetch(pieces, refs, weight, semaphores)
    lane_q = lane_of(rows)
    lane_k = lane_of(keys)
    ext_k = ext_k_ref[...]
    pair = contract(normed_ref[...], weight[:, : 2 * width], 1, 0) + bias_ref[:, : 2 * width]
    pair = pair.astype(LOW)
    query = contract(normed_ref[:rows, :], weight[:, 2 * width :], 1, 0) + bias_ref[:, 2 * width :]
    query = (query.astype(LOW).astype(FULL) * HEAD_DIM**-0.5).astype(LOW)
    for head in range(heads):
        at = head * HEAD_DIM
        q_ref[head] = jnp.where(lane_q < HEAD_DIM, spread(query, width + at), ext_q_ref[...])
        k_ref[head] = jnp.where(lane_k < HEAD_DIM, spread(pair, at), ext_k)
        v_ref[head] = jnp.where(lane_k < HEAD_DIM, spread(pair, width + at), ext_k)
    saves = [
        pltpu.make_async_copy(source, target, leaving.at[at])
        for at, (source, target) in enumerate(
            ((k_ref, k_out), (v_ref, v_out), (q_ref, q_out), (mixed_ref, mixed_out))
        )
    ]
    saves[0].start()
    saves[1].start()
    for head in range(heads):
        scores = contract(q_ref[head], k_ref[head], 1, 1)
        highest = jnp.max(scores, axis=1, keepdims=True)
        weights = jnp.exp(scores - highest)
        total = jnp.sum(weights, axis=1, keepdims=True)
        mixed = contract(weights.astype(LOW), v_ref[head], 1, 0) / total
        mixed_ref[:, head * HEAD_DIM : (head + 1) * HEAD_DIM] = mixed[:, :HEAD_DIM].astype(LOW)
        pieces = pieces_of(-(highest + jnp.log(total)))
        q_ref[head] = put_pieces(lane_q, HEAD_DIM, pieces, q_ref[head])
    saves[2].start()
    saves[3].start()
    answer = contract(mixed_ref[...], weight[:, 2 * width : 3 * width], 1, 1)
    out_ref[...] = acc_ref[...] + answer if started else answer
    for save in saves:
        save.wait()


def attend(normed, source, bias, ext_q, ext_k, acc, heads):
    arrays, pieces = source
    rows, keys = ext_q.shape[0], ext_k.shape[0]
    model = normed.shape[1]
    saved = [
        ((rows, heads * HEAD_DIM), LOW),
        ((heads, rows, LANES), LOW),
        ((heads, keys, LANES), LOW),
        ((heads, keys, LANES), LOW),
    ]

    def kernel(*refs):
        attend_kernel(heads, rows, keys, pieces, acc is not None, *refs)

    start = [] if acc is None else [acc]
    return pl.pallas_call(
        kernel,
        out_shape=(
            jax.ShapeDtypeStruct((rows, model), FULL),
            *(pltpu.HBM(*item) for item in saved),
        ),
        in_specs=[WHOLE] * (4 + len(start)) + [ANYWHERE] * len(arrays),
        out_specs=(WHOLE,) + (ANYWHERE,) * 4,
        input_output_aliases={4: 0} if start else {},
        scratch_shapes=[
            pltpu.VMEM((model, arrays[0].shape[1]), LOW),
            *(pltpu.VMEM(*item) for item in saved),
            pltpu.SemaphoreType.DMA((len(pieces),)),
            pltpu.SemaphoreType.DMA((4,)),
        ],
        cost_estimate=pl.CostEstimate(
            flops=4 * heads * rows * keys * LANES + 8 * rows * model * heads * HEAD_DIM,
            transcendentals=heads * rows * keys,
            bytes_accessed=2 * (normed.size + 4 * rows * model + 8 * rows * heads * LANES),
        ),
        compiler_params=pltpu.CompilerParams(vmem_limit_bytes=14 << 20),
        name="attend",
    )(normed, bias, ext_q, ext_k, *start, *outside(arrays))


def mlp_kernel(
    block, pieces, place, started,
    normed_ref, normed_t_ref, seed_ref, seed_t_ref, bias_ref, *refs
):
    if started:
        out_in_ref, d_in_ref, *refs = refs
    out_ref, d_ref, kept_out, sent_out, sums_ref = refs[-10:-5]
    weight, kept_ref, sent_ref, semaphores, leaving = refs[-5:]
    cut = kept_ref.shape[0]
    units = bias_ref.shape[1]

    def spans(at):
        return (
            pl.ds(pl.multiple_of(at * block, block), block),
            pl.ds(pl.multiple_of(units + at * block, block), block),
        )

    def copies(at):
        return [
            pltpu.make_async_copy(
                refs[source].at[pl.ds(start, count), span],
                weight.at[pl.ds(put, count), span],
                semaphores.at[at, 2 * order + side],
            )
            for order, (source, start, put, count) in enumerate(pieces)
            for side, span in enumerate(spans(at))
        ]

    def saves(at):
        return [
            pltpu.make_async_copy(
                source.at[:, span], target.at[place, :, span], leaving.at[at, 2 * order + side]
            )
            for order, (source, target) in enumerate(((kept_ref, kept_out), (sent_ref, sent_out)))
            for side, span in enumerate(spans(at))
        ]

    for at in range(units // block):
        for copy in copies(at):
            copy.start()
    out_ref[...] = out_in_ref[...] if started else jnp.zeros(out_ref.shape, FULL)
    d_ref[...] = d_in_ref[...] if started else jnp.zeros(d_ref.shape, FULL)

    def step(at, carry):
        span_up, span_down = spans(at)
        for copy in copies(at):
            copy.wait()
        up = contract(normed_ref[...], weight[:, span_up], 1, 0) + bias_ref[:, span_up]
        d_active = contract(seed_ref[...], weight[:, span_down], 1, 0)
        cumulative = 0.5 + 0.5 * lax.erf(up * 0.7071067811865476)
        active = (up * cumulative).astype(LOW)
        slope = cumulative + up * (jnp.exp(-0.5 * up * up) * 0.3989422804014327)
        d_up = (d_active * slope).astype(LOW)
        sums_ref[:, span_up] = jnp.sum(d_up.astype(FULL), axis=0, keepdims=True)
        out_ref[...] += contract(active, weight[:, span_down], 1, 1)
        d_ref[...] += contract(d_up, weight[:, span_up], 1, 1)
        grad_up = contract(normed_t_ref[...], d_up, 1, 0).astype(LOW)
        kept_ref[:, span_up] = grad_up[:cut]
        sent_ref[:, span_up] = grad_up[cut:]
        grad_down = contract(seed_t_ref[...], active, 1, 0).astype(LOW)
        kept_ref[:, span_down] = grad_down[:cut]
        sent_ref[:, span_down] = grad_down[cut:]
        for save in saves(at):
            save.start()
        return carry

    lax.fori_loop(0, units // block, step, 0)
    for at in range(units // block):
        for save in saves(at):
            save.wait()


def mlp(normed, normed_t, seed, seed_t, source, bias, out, d_normed, grads, at, total):
    arrays, pieces = source
    rows, model = normed.shape
    units = bias.shape[1]
    cut = model // 2

    def kernel(*refs):
        mlp_kernel(256, pieces, at, out is not None, *refs)

    grad_shape = pltpu.HBM((total, cut, 2 * units), LOW)
    grads = list(grads)
    start = [] if out is None else [out, d_normed]
    first = 5 + len(start) + len(arrays)
    return pl.pallas_call(
        kernel,
        out_shape=(
            jax.ShapeDtypeStruct((rows, model), FULL),
            jax.ShapeDtypeStruct((rows, model), FULL),
            grad_shape,
            grad_shape,
            jax.ShapeDtypeStruct((1, units), FULL),
        ),
        in_specs=[WHOLE] * (5 + len(start)) + [ANYWHERE] * (len(arrays) + len(grads)),
        out_specs=(WHOLE, WHOLE, ANYWHERE, ANYWHERE, WHOLE),
        input_output_aliases={
            **({5: 0, 6: 1} if start else {}),
            **({first: 2, first + 1: 3} if grads else {}),
        },
        scratch_shapes=[
            pltpu.VMEM((model, 2 * units), LOW),
            pltpu.VMEM((cut, 2 * units), LOW),
            pltpu.VMEM((cut, 2 * units), LOW),
            pltpu.SemaphoreType.DMA((units // 256, 2 * len(pieces))),
            pltpu.SemaphoreType.DMA((units // 256, 4)),
        ],
        cost_estimate=pl.CostEstimate(
            flops=12 * rows * model * units,
            transcendentals=2 * rows * units,
            bytes_accessed=16 * rows * model + 8 * model * units,
        ),
        compiler_params=pltpu.CompilerParams(vmem_limit_bytes=14 << 20),
        name="mlp",
    )(normed, normed_t, seed, seed_t, bias, *start, *outside(arrays), *outside(grads))


def back_kernel(
    heads, rows, keys, pieces, started, d_ref, d_t_ref, normed_t_ref, *refs
):
    if started:
        own_in_ref, other_in_ref, *refs = refs
    q_in, k_in, v_in, mixed_in, *refs = refs
    own_ref, other_ref, kept_out, sent_out, sums_ref = refs[-19:-14]
    (
        weight, q_ref, k_ref, v_ref, mixed_ref, kept_ref, sent_ref,
        u_buf, dq_buf, dk_buf, dv_buf, pair_buf, query_buf, semaphores,
    ) = refs[-14:]
    width = heads * HEAD_DIM
    cut = kept_ref.shape[0]
    first = len(pieces)
    entering = [
        pltpu.make_async_copy(source, target, semaphores.at[first + at])
        for at, (source, target) in enumerate(
            ((mixed_in, mixed_ref), (q_in, q_ref), (k_in, k_ref), (v_in, v_ref))
        )
    ]
    for copy in entering:
        copy.start()
    fetch(pieces, refs, weight, semaphores)
    lane_q = lane_of(rows)
    upstream_all = contract(d_ref[...], weight[:, 2 * width : 3 * width], 1, 0).astype(LOW)
    entering[0].wait()
    mixed = mixed_ref[...]
    for head in range(heads):
        at = head * HEAD_DIM
        product = upstream_all[:, at : at + HEAD_DIM].astype(FULL) * mixed[
            :, at : at + HEAD_DIM
        ].astype(FULL)
        pieces_here = pieces_of(-jnp.sum(product, axis=1, keepdims=True))
        rest = jnp.where(lane_q < HEAD_DIM, spread(upstream_all, at), jnp.zeros((), LOW))
        u_buf[head] = put_pieces(lane_q, HEAD_DIM, pieces_here, rest)
    for copy in entering[1:]:
        copy.wait()
    block = 256

    def one_head(head, carry):
        queries = q_ref[head]
        upstream = u_buf[head]
        total = jnp.zeros((rows, LANES), FULL)
        for start in range(0, keys, block):
            span = pl.ds(start, block)
            keys_part = k_ref[head, span, :]
            shares = jnp.exp(contract(keys_part, queries, 1, 1))
            d_scores = (shares * contract(v_ref[head, span, :], upstream, 1, 1)).astype(LOW)
            dv_buf[head, span, :] = contract(shares.astype(LOW), upstream, 1, 0).astype(LOW)
            dk_buf[head, span, :] = contract(d_scores, queries, 1, 0).astype(LOW)
            total = total + contract(d_scores, keys_part, 0, 0)
        dq_buf[head] = (total * HEAD_DIM**-0.5).astype(LOW)
        return carry

    lax.fori_loop(0, heads, one_head, 0)
    query_buf[:, :width] = jnp.zeros((rows, width), LOW)
    for head in range(heads):
        at = head * HEAD_DIM
        query_buf[:, width + at : width + at + HEAD_DIM] = dq_buf[head][:, :HEAD_DIM]
        pair_buf[:, at : at + HEAD_DIM] = dk_buf[head][:, :HEAD_DIM]
        pair_buf[:, width + at : width + at + HEAD_DIM] = dv_buf[head][:, :HEAD_DIM]
    grad_pair = contract(normed_t_ref[...], pair_buf[...], 1, 0).astype(LOW)
    kept_ref[:, : 2 * width] = grad_pair[:cut]
    sent_ref[:, : 2 * width] = grad_pair[cut:]
    grad_query = contract(normed_t_ref[:, :rows], query_buf[...], 1, 0).astype(LOW)
    kept_ref[:, 2 * width :] = grad_query[:cut]
    sent_ref[:, 2 * width :] = grad_query[cut:]
    grad_out = contract(d_t_ref[...], mixed, 1, 0).astype(LOW)
    kept_ref[:, 2 * width : 3 * width] = grad_out[:cut]
    sent_ref[:, 2 * width : 3 * width] = grad_out[cut:]
    saves = [
        pltpu.make_async_copy(kept_ref, kept_out, semaphores.at[first + 4]),
        pltpu.make_async_copy(sent_ref, sent_out, semaphores.at[first + 5]),
    ]
    for save in saves:
        save.start()
    sums_ref[:, : 2 * width] = jnp.sum(pair_buf[...].astype(FULL), axis=0, keepdims=True)
    sums_ref[:, 2 * width :] = jnp.sum(query_buf[...].astype(FULL), axis=0, keepdims=True)
    own = contract(pair_buf[:rows, :], weight[:, : 2 * width], 1, 1) + contract(
        query_buf[...], weight[:, 2 * width :], 1, 1
    )
    own_ref[...] = own_in_ref[...] + own if started else own
    other = contract(pair_buf[rows:, :], weight[:, : 2 * width], 1, 1)
    other_ref[...] = (other_in_ref[...] + other if started else other).astype(other_ref.dtype)
    for save in saves:
        save.wait()


def attend_back(d_middle, d_middle_t, normed_t, source, saved, own, other, heads, last):
    arrays, pieces = source
    mixed, queries, keys_all, values = saved
    rows, keys = d_middle.shape[0], normed_t.shape[1]
    model = normed_t.shape[0]
    cut, columns = model // 2, arrays[0].shape[1]
    width = heads * HEAD_DIM

    def kernel(*refs):
        back_kernel(heads, rows, keys, pieces, own is not None, *refs)

    start = [] if own is None else [own, other]
    aliases = {3: 0, 4: 1} if start else {}
    if last:
        aliases.pop(4)
    return pl.pallas_call(
        kernel,
        out_shape=(
            jax.ShapeDtypeStruct((rows, model), FULL),
            jax.ShapeDtypeStruct((rows, model), LOW if last else FULL),
            pltpu.HBM((cut, columns), LOW),
            pltpu.HBM((cut, columns), LOW),
            jax.ShapeDtypeStruct((1, columns), FULL),
        ),
        in_specs=[WHOLE] * (3 + len(start)) + [ANYWHERE] * (4 + len(arrays)),
        out_specs=(WHOLE, WHOLE, ANYWHERE, ANYWHERE, WHOLE),
        input_output_aliases=aliases,
        scratch_shapes=[
            pltpu.VMEM((model, columns), LOW),
            pltpu.VMEM((heads, rows, LANES), LOW),
            pltpu.VMEM((heads, keys, LANES), LOW),
            pltpu.VMEM((heads, keys, LANES), LOW),
            pltpu.VMEM((rows, width), LOW),
            pltpu.VMEM((cut, columns), LOW),
            pltpu.VMEM((cut, columns), LOW),
            pltpu.VMEM((heads, rows, LANES), LOW),
            pltpu.VMEM((heads, rows, LANES), LOW),
            pltpu.VMEM((heads, keys, LANES), LOW),
            pltpu.VMEM((heads, keys, LANES), LOW),
            pltpu.VMEM((keys, 2 * width), LOW),
            pltpu.VMEM((rows, columns - 2 * width), LOW),
            pltpu.SemaphoreType.DMA((len(pieces) + 6,)),
        ],
        cost_estimate=pl.CostEstimate(
            flops=10 * heads * rows * keys * LANES + 20 * rows * model * width,
            transcendentals=heads * rows * keys,
            bytes_accessed=8 * keys * model + 8 * rows * model,
        ),
        compiler_params=pltpu.CompilerParams(vmem_limit_bytes=16 << 20),
        name="attend_back",
    )(
        d_middle, d_middle_t, normed_t, *start,
        *outside((queries, keys_all, values, mixed)), *outside(arrays),
    )


def call_rows(kernel, shapes, *arrays):
    return pl.pallas_call(
        kernel,
        out_shape=tuple(jax.ShapeDtypeStruct(*shape) for shape in shapes),
        in_specs=[WHOLE] * len(arrays),
        out_specs=(WHOLE,) * len(shapes),
        cost_estimate=pl.CostEstimate(
            flops=2 * arrays[0].size * arrays[0].shape[1],
            transcendentals=0,
            bytes_accessed=sum(array.size * array.dtype.itemsize for array in arrays),
        ),
        compiler_params=pltpu.CompilerParams(vmem_limit_bytes=12 << 20),
    )(*arrays)


def pack_kernel(
    rows, spots_ref, gains_ref, shifts_ref, heads_ref, ups_ref, labels_ref, out_ref, line
):
    at = 0
    for ref in (gains_ref, shifts_ref, heads_ref, ups_ref):
        count, size = ref.shape
        for which in range(count):
            line[:, at : at + size] = ref[which : which + 1, :].astype(FULL)
            at += size
    start = pl.multiple_of(spots_ref[2], LANES)
    line[:, at:] = labels_ref[pl.ds(spots_ref[1], 1), pl.ds(start, rows)].astype(FULL)
    place = lax.broadcasted_iota(jnp.int32, out_ref.shape, 0) == spots_ref[0]
    out_ref[...] = jnp.where(place, jnp.broadcast_to(line[...], out_ref.shape), 0.0).astype(LOW)


def pack_small(spots, devices, rows, *arrays):
    size = sum(array.size for array in arrays[:-1]) + rows

    def kernel(*refs):
        pack_kernel(rows, *refs)

    return pl.pallas_call(
        kernel,
        out_shape=jax.ShapeDtypeStruct((devices, size), LOW),
        in_specs=[pl.BlockSpec(memory_space=pltpu.SMEM)] + [WHOLE] * len(arrays),
        out_specs=WHOLE,
        scratch_shapes=[pltpu.VMEM((1, size), FULL)],
        compiler_params=pltpu.CompilerParams(vmem_limit_bytes=4 << 20),
        name="pack_small",
    )(spots, *arrays)


def pick_kernel(starts_ref, sums_ref, gains_ref, shifts_ref, heads_ref, ups_ref):
    total = sums_ref.shape[1]

    def window(first, count, which, size):
        moved = pltpu.roll(sums_ref[...], (total - starts_ref[which]) % total, 1)
        return moved[first : first + count, :size]

    fine, piece, unit = gains_ref.shape[1], heads_ref.shape[1], ups_ref.shape[1]
    gains_ref[...] = window(0, 2, 0, fine)
    shifts_ref[...] = window(2, 4, 0, fine)
    heads_ref[0:1, :] = window(6, 1, 2, piece)
    heads_ref[1:2, :] = window(6, 1, 1, piece)
    ups_ref[...] = window(7, 1, 3, unit)


def pick_own(starts, sums, fine, piece, unit):
    return pl.pallas_call(
        pick_kernel,
        out_shape=tuple(
            jax.ShapeDtypeStruct(shape, FULL)
            for shape in ((2, fine), (4, fine), (2, piece), (1, unit))
        ),
        in_specs=[pl.BlockSpec(memory_space=pltpu.SMEM), WHOLE],
        compiler_params=pltpu.CompilerParams(vmem_limit_bytes=4 << 20),
        name="pick_own",
    )(starts, sums)


def enter_kernel(rows_ref, shuffle_ref, out_ref, out_t_ref):
    moved = contract(rows_ref[...], shuffle_ref[...], 1, 0).astype(LOW)
    out_ref[...] = moved
    out_t_ref[...] = moved.T


def first_norm_kernel(rows_ref, shuffle_ref, norm_ref, rows_out, normed_ref):
    moved = contract(rows_ref[...], shuffle_ref[...], 1, 0)
    rows_out[...] = moved.astype(LOW)
    normed_ref[...] = normalize(moved, norm_ref[0:1, :], norm_ref[2:3, :])[0].astype(LOW)


def both_kernel(own_ref, other_ref, both_ref, both_t_ref):
    rows, model = own_ref.shape
    cut = model // 2
    both_ref[:rows, :] = own_ref[...]
    both_ref[rows:, :cut] = other_ref[:, cut:]
    both_ref[rows:, cut:] = other_ref[:, :cut]
    both_t_ref[...] = both_ref[...].T


def second_norm_kernel(rows_ref, attended_ref, norm_ref, middle_ref, normed_ref, normed_t_ref):
    middle = rows_ref[...].astype(FULL) + attended_ref[...] + norm_ref[4:5, :]
    middle_ref[...] = middle
    normed = normalize(middle, norm_ref[1:2, :], norm_ref[3:4, :])[0].astype(LOW)
    normed_ref[...] = normed
    normed_t_ref[...] = normed.T


def add_up(array):
    return jnp.sum(array, axis=0, keepdims=True)


def second_back_kernel(
    middle_ref, d_normed_ref, seed_ref, mlp_ref, norm_ref, shuffle_ref,
    d_ref, d_low_ref, d_t_ref, result_ref, sums_ref,
):
    middle = middle_ref[...]
    _, unit, inverse = normalize(middle, norm_ref[1:2, :], norm_ref[3:4, :])
    d_normed = d_normed_ref[...]
    seed = seed_ref[...].astype(FULL)
    d_middle = seed + norm_back(d_normed, unit, inverse, norm_ref[1:2, :])
    d_ref[...] = d_middle
    low = d_middle.astype(LOW)
    d_low_ref[...] = low
    d_t_ref[...] = low.T
    sums_ref[0:1, :] = add_up(d_normed * unit)
    sums_ref[1:2, :] = add_up(d_normed)
    sums_ref[2:3, :] = add_up(d_middle)
    sums_ref[3:4, :] = add_up(seed)
    result = (middle + mlp_ref[...] + norm_ref[5:6, :]).astype(LOW)
    result_ref[...] = contract(result, shuffle_ref[...], 1, 1).astype(LOW)


def first_back_kernel(
    rows_ref, own_ref, other_ref, d_middle_ref, norm_ref, shuffle_ref, d_rows_ref, sums_ref
):
    cut = own_ref.shape[1] // 2
    _, unit, inverse = normalize(rows_ref[...].astype(FULL), norm_ref[0:1, :], norm_ref[2:3, :])
    other = jnp.concatenate([other_ref[:, cut:], other_ref[:, :cut]], axis=1)
    d_normed = own_ref[...] + other.astype(FULL)
    d_rows = d_middle_ref[...] + norm_back(d_normed, unit, inverse, norm_ref[0:1, :])
    d_rows_ref[...] = contract(d_rows.astype(LOW), shuffle_ref[...], 1, 1).astype(LOW)
    sums_ref[0:1, :] = add_up(d_normed * unit)
    sums_ref[1:2, :] = add_up(d_normed)


def build(fsdp, tp):
    bits = fsdp.bit_length() - 1
    tp_bits = tp.bit_length() - 1
    masks = sorted(range(fsdp), key=lambda mask: (mask & 1, mask >> 1))

    def flip(array, bit):
        return lax.ppermute(array, "fsdp", [(at, at ^ (1 << bit)) for at in range(fsdp)])

    def flip_tp(array, bit):
        return lax.ppermute(array, "tp", [(at, at ^ (1 << bit)) for at in range(tp)])

    def trade_rows(array):
        pairs = []
        for row in range(fsdp):
            for column in range(tp):
                odd = (row ^ column) & 1
                pairs.append((row * tp + column, (row ^ odd) * tp + (column ^ odd)))
        return lax.ppermute(array, ("fsdp", "tp"), pairs)

    def sum_everywhere(array):
        for bit in range(bits):
            arrived = flip(array, bit)
            array = array + arrived
        for bit in range(tp_bits):
            arrived = flip_tp(array, bit)
            array = array + arrived
        return array

    def order_of(slot):
        upper = list(range(1, bits))
        return upper if slot % 2 == 0 else upper[::-1]

    def gather_rows(current, count, turn):
        rows = current.shape[0] // count
        order = order_of(turn)
        held = [(0, at) for at in range(count)]
        for bit in order[:-1]:
            both = held + [(mask ^ (1 << bit), at) for mask, at in held]
            arrived = flip(current, bit)
            current, held = join([current, arrived]), both
        last = order[-1]
        arrived = flip(current, last)
        found = [(current, held), (arrived, [(mask ^ (1 << last), at) for mask, at in held])]
        if rows % 16:
            wanted = sorted(found[0][1] + found[1][1], key=lambda item: (item[1], item[0]))
            cut = {}
            for array, items in found:
                for spot, item in enumerate(items):
                    cut[item] = array[spot * rows : (spot + 1) * rows]
            found = [(jnp.concatenate([cut[item] for item in wanted], axis=0), wanted)]
        found += [(flip(array, 0), [(mask ^ 1, at) for mask, at in items]) for array, items in found]
        arrays = [array for array, _ in found]
        sources = []
        for at in range(count):
            pieces = []
            for index, (_, items) in enumerate(found):
                for spot, (mask, shard) in enumerate(items):
                    if shard != at:
                        continue
                    start, put = spot * rows, masks.index(mask) * rows
                    if pieces:
                        source, before, place, length = pieces[-1]
                        if (source, before + length, place + length) == (index, start, put):
                            pieces[-1] = (source, before, place, length + rows)
                            continue
                    pieces.append((index, start, put, rows))
            sources.append((arrays, pieces))
        return sources

    def scatter_rows(kept, sent, turn):
        arrived = flip(sent, 0)
        terms = [kept, arrived]
        held = [mask for mask in masks if not mask & 1]
        rows = kept.shape[-2] // len(held)

        def pick(array, positions):
            if positions == list(range(positions[0], positions[0] + len(positions))):
                return array[..., positions[0] * rows : (positions[-1] + 1) * rows, :]
            return jnp.concatenate(
                [array[..., at * rows : (at + 1) * rows, :] for at in positions], axis=-2
            )

        for bit in order_of(turn)[::-1]:
            stay = [at for at, mask in enumerate(held) if not mask >> bit & 1]
            leave = [at for at, mask in enumerate(held) if mask >> bit & 1]
            leaving = total_of([pick(term, leave) for term in terms]).astype(LOW)
            arrived = flip(leaving, bit)
            terms = [pick(term, stay) for term in terms] + [arrived]
            held = [held[at] for at in stay]
        return terms

    def spread_tp(shard):
        slots = [shard]
        for bit in range(tp_bits):
            for at in range(1 << bit):
                slots.append(flip_tp(slots[at], bit))
        return slots

    def local(
        frames, segments, w_qkv, w_out, w_up, w_down, head_bias, up_bias, ln_gains, shifts, cotangent
    ):
        row = lax.axis_index("fsdp")
        column = lax.axis_index("tp")
        rows, model = frames.shape
        block = model // fsdp
        width = w_qkv.shape[2]
        heads = width // HEAD_DIM
        units = w_up.shape[1]
        fine = ln_gains.shape[1]

        parts = [w_qkv[:, 1], w_qkv[:, 2], w_out.T, w_qkv[:, 0]]
        first_shard = jnp.concatenate(parts, axis=1)
        second_shard = jnp.concatenate([w_up, w_down.T], axis=1)
        first_parts = spread_tp(first_shard)
        pairs = [join(first_parts[at : at + 2]) for at in range(0, tp, 2)]
        first_slots = []
        for at, pair in enumerate(pairs):
            first_slots += gather_rows(pair, 2, at)
        second_slots = []
        for slot, shard in enumerate(spread_tp(second_shard)):
            second_slots += gather_rows(shard, 1, 2 * slot // tp)

        here = tp // segments.shape[0]
        spots = jnp.stack([row * tp + column, column // here, column % here * rows])
        small = sum_everywhere(
            pack_small(
                spots, fsdp * tp, rows,
                ln_gains, shifts, head_bias, up_bias.reshape(1, -1), segments,
            )
        )
        cut = 6 * fine
        norm_rows = small[:, :cut].reshape(fsdp * tp, 6, fine).transpose(1, 0, 2).reshape(6, model)
        piece = head_bias.shape[1]
        head_rows = small[:, cut : cut + 2 * piece].reshape(fsdp, tp, 2, piece)
        head_rows = head_rows.transpose(1, 2, 0, 3).reshape(tp, 2, width).astype(FULL)
        up_rows = small[:, cut + 2 * piece : -rows].reshape(fsdp, tp, up_bias.shape[0])
        up_rows = up_rows.transpose(1, 0, 2).reshape(tp, 1, units).astype(FULL)

        out_at = lax.broadcasted_iota(jnp.int32, (model, model), 1)
        in_at = lax.broadcasted_iota(jnp.int32, (model, model), 0)
        spot = out_at // block
        mask_at = ((spot & (fsdp // 2 - 1)) << 1) | (spot >> (bits - 1))
        shuffle = (in_at == (row ^ mask_at) * block + out_at % block).astype(LOW)

        norm_rows = contract(norm_rows, shuffle, 1, 0)
        first_row = ((row & -2) | (column & 1)) * tp + (column & -2)

        def labels_of(half):
            found = lax.dynamic_index_in_dim(small, first_row + half, 0, keepdims=False)
            return found[-rows:].astype(jnp.int32)

        own_labels, other_labels = labels_of(row & 1), labels_of(1 - (row & 1))
        all_labels = jnp.concatenate([own_labels, other_labels])

        def extension(labels_part, lead, marks):
            lane = lane_of(labels_part.shape[0])
            clip = lane - (HEAD_DIM + 3)
            values = jnp.where((clip >= 0) & (clip < CLIPS), marks(clip == labels_part[:, None]), 0.0)
            is_lead = (lane >= HEAD_DIM) & (lane < HEAD_DIM + 3)
            return jnp.where(is_lead, lead, values).astype(LOW)

        ext_q = extension(own_labels, 0.0, lambda same: jnp.where(same, 0.0, MASKED))
        ext_k = extension(all_labels, 1.0, lambda same: jnp.where(same, 1.0, 0.0))

        tall = (rows, model)
        wide = (model, rows)
        local_rows, first_low = call_rows(
            first_norm_kernel, ((tall, LOW), (tall, LOW)),
            trade_rows(frames), shuffle, norm_rows,
        )
        first_both, first_t = call_rows(
            both_kernel, (((2 * rows, model), LOW), ((model, 2 * rows), LOW)),
            first_low, flip(first_low, 0),
        )
        seed = trade_rows(cotangent)
        upstream_low, upstream_t = call_rows(
            enter_kernel, ((tall, LOW), (wide, LOW)), seed, shuffle
        )

        def slot_row(array, slot):
            return lax.dynamic_index_in_dim(array, column ^ slot, 0, keepdims=False)

        saved = []
        attended = None
        none = jnp.zeros((width,), FULL)
        for slot in range(tp):
            bias = slot_row(head_rows, slot)
            bias = jnp.concatenate([none, bias[1], none, bias[0]])[None]
            attended, *kept = attend(
                first_both, first_slots[slot], bias, ext_q, ext_k, attended, heads
            )
            saved.append(kept)
        middle, second_low, second_t = call_rows(
            second_norm_kernel, ((tall, FULL), (tall, LOW), (wide, LOW)),
            local_rows, attended, norm_rows,
        )

        mlp_out = d_second = None
        grad_second, unit_sums, grads = [], [], ()
        for slot in range(tp):
            mlp_out, d_second, *grads, sums = mlp(
                second_low, second_t, upstream_low, upstream_t, second_slots[slot],
                slot_row(up_rows, slot), mlp_out, d_second, grads, slot % 2, 2,
            )
            unit_sums.append(sums)
            if slot % 2:
                grad_second.append(scatter_rows(*grads, slot // 2))
                grads = ()
        d_middle, d_middle_low, d_middle_t, result, early_sums = call_rows(
            second_back_kernel,
            ((tall, FULL), (tall, LOW), (wide, LOW), (tall, LOW), ((4, model), FULL)),
            middle, d_second, upstream_low, mlp_out, norm_rows, shuffle,
        )
        result = trade_rows(result)

        def sum_tp(parts):
            for bit in range(tp_bits):
                for slot in range(tp - (1 << bit), 0, -(2 << bit)):
                    arrived = flip_tp(total_of(parts[slot]).astype(LOW), bit)
                    parts[slot ^ (1 << bit)] = parts[slot ^ (1 << bit)] + [arrived]
            return total_of(parts[0])

        grad_first = [None] * tp
        head_sums = [None] * tp
        d_own = d_other = None
        for slot in range(tp - 1, -1, -1):
            d_own, d_other, kept, sent, sums = attend_back(
                d_middle_low, d_middle_t, first_t, first_slots[slot], saved[slot],
                d_own, d_other, heads, slot == 0,
            )
            grad_first[slot] = scatter_rows(kept, sent, slot)
            head_sums[slot] = sums
        d_rows, late_sums = call_rows(
            first_back_kernel, ((tall, LOW), ((2, model), FULL)),
            local_rows, d_own, flip(d_other, 0), d_middle, norm_rows, shuffle,
        )
        d_rows = trade_rows(d_rows)

        sums = jnp.concatenate(
            [late_sums[:1], early_sums[:1], late_sums[1:], early_sums[1:]], axis=0
        )
        sums = lax.dot_general(
            sums,
            shuffle.astype(FULL),
            (((1,), (1,)), ((), ())),
            precision=lax.Precision.HIGHEST,
            preferred_element_type=FULL,
        )
        packed = jnp.concatenate(
            [sums] + [item for pair in zip(head_sums, unit_sums) for item in pair], axis=0
        )
        for bit in range(tp_bits - 1, -1, -1):
            keep = 6 + 2 * (1 << bit)
            arrived = flip_tp(jnp.concatenate([packed[:6], packed[keep:]], axis=0), bit)
            packed = packed[:keep] + arrived
        for bit in range(bits):
            packed = packed + flip(packed, bit)
        starts = jnp.stack(
            [(row * tp + column) * fine, width + row * piece, 3 * width + row * piece, row * up_bias.shape[0]]
        )
        gain_grads, shift_grads, grad_headbias, grad_upbias = pick_own(
            starts, packed, fine, piece, up_bias.shape[0]
        )
        grad_upbias = grad_upbias[0]

        total_first = sum_tp(grad_first)
        total_second = sum_tp([[term[at % 2] for term in grad_second[at // 2]] for at in range(tp)])
        total_qkv = [total_first[:, at * width : (at + 1) * width] for at in (3, 0, 1)]
        return (
            result,
            d_rows,
            jnp.stack(total_qkv, axis=1),
            total_first[:, 2 * width : 3 * width].T,
            total_second[:, :units],
            total_second[:, units:].T,
            grad_headbias,
            grad_upbias,
            gain_grads,
            shift_grads,
        )

    return local


def solution(mesh):
    placed = (
        P(("fsdp", "tp"), None),
        P("fsdp", None),
        P("fsdp", None, "tp"),
        P("tp", "fsdp"),
        P("fsdp", "tp"),
        P("tp", "fsdp"),
        P(None, ("tp", "fsdp")),
        P(("tp", "fsdp")),
        P(None, ("fsdp", "tp")),
        P(None, ("fsdp", "tp")),
        P(("fsdp", "tp"), None),
    )
    body = build(mesh.shape["fsdp"], mesh.shape["tp"])

    return jax.shard_map(
        body,
        mesh=mesh,
        in_specs=placed,
        out_specs=(
            P(("fsdp", "tp"), None),
            P(("fsdp", "tp"), None),
            P("fsdp", None, "tp"),
            P("tp", "fsdp"),
            P("fsdp", "tp"),
            P("tp", "fsdp"),
            P(None, ("tp", "fsdp")),
            P(("tp", "fsdp")),
            P(None, ("fsdp", "tp")),
            P(None, ("fsdp", "tp")),
        ),
        check_vma=False,
    )
```

```python
import jax
import jax.numpy as jnp
from jax import lax
from jax.experimental import pallas as pl
from jax.experimental.pallas import tpu as pltpu
from jax.sharding import PartitionSpec as P


HEAD_DIM = 64
LANES = 128
CLIPS = 3
EPSILON = 1e-05
MASKED = -1000000000.0
LOW = jnp.bfloat16
FULL = jnp.float32


def normalize(values, gain_row, shift_row):
    average = jnp.mean(values, axis=-1, keepdims=True)
    centered = values - average
    inverse = lax.rsqrt(jnp.mean(centered * centered, axis=-1, keepdims=True) + EPSILON)
    normed = centered * inverse
    return (normed * gain_row + shift_row, normed, inverse)


def norm_back(incoming, normed, inverse, gain_row):
    scaled = incoming * gain_row
    return inverse * (
        scaled
        - jnp.mean(scaled, axis=-1, keepdims=True)
        - normed * jnp.mean(scaled * normed, axis=-1, keepdims=True)
    )


def contract(left, right, left_dim, right_dim):
    return lax.dot_general(
        left, right, (((left_dim,), (right_dim,)), ((), ())), preferred_element_type=FULL
    )


def pieces_of(column):
    high = column.astype(LOW)
    rest = column - high.astype(FULL)
    middle = rest.astype(LOW)
    low = (rest - middle.astype(FULL)).astype(LOW)
    return high, middle, low


def lane_of(rows):
    return lax.broadcasted_iota(jnp.int32, (rows, LANES), 1)


def spread(ref_value, start):
    half = ref_value[:, start : start + HEAD_DIM]
    return jnp.concatenate([half, half], axis=1)


def put_pieces(lane, base, pieces, rest):
    for step, piece in enumerate(pieces):
        rest = jnp.where(lane == base + step, piece, rest)
    return rest


def total_of(terms):
    total = terms[0].astype(FULL)
    for term in terms[1:]:
        total = total + term.astype(FULL)
    return total


ANYWHERE = pl.BlockSpec(memory_space=pltpu.HBM)
WHOLE = pl.BlockSpec(memory_space=pltpu.VMEM)


def outside(arrays):
    return [pltpu.with_memory_space_constraint(array, pltpu.HBM) for array in arrays]


def run_copies(moves, semaphores):
    copies = [
        pltpu.make_async_copy(source, target, semaphores.at[at])
        for at, (source, target) in enumerate(moves)
    ]
    for copy in copies:
        copy.start()
    for copy in copies:
        copy.wait()


def fetch(pieces, refs, target, semaphores):
    run_copies(
        [
            (refs[source].at[pl.ds(start, count)], target.at[pl.ds(put, count)])
            for source, start, put, count in pieces
        ],
        semaphores,
    )


def join(arrays):
    rows, columns = arrays[0].shape
    if rows % 16:
        return jnp.concatenate(arrays, axis=0)
    count = len(arrays)

    def kernel(*refs):
        for at in range(count):
            refs[count][at * rows : (at + 1) * rows, :] = refs[at][...]

    return pl.pallas_call(
        kernel,
        out_shape=jax.ShapeDtypeStruct((count * rows, columns), arrays[0].dtype),
        cost_estimate=pl.CostEstimate(
            flops=0, transcendentals=0, bytes_accessed=4 * count * rows * columns
        ),
        compiler_params=pltpu.CompilerParams(vmem_limit_bytes=6 << 20),
        name="join",
    )(*arrays)


def attend_kernel(
    heads, rows, keys, pieces, started, normed_ref, bias_ref, ext_q_ref, ext_k_ref, *refs
):
    if started:
        acc_ref, *refs = refs
    out_ref, mixed_out, q_out, k_out, v_out = refs[-12:-7]
    weight, mixed_ref, q_ref, k_ref, v_ref, semaphores, leaving = refs[-7:]
    width = heads * HEAD_DIM
    fetch(pieces, refs, weight, semaphores)
    lane_q = lane_of(rows)
    lane_k = lane_of(keys)
    ext_k = ext_k_ref[...]
    pair = contract(normed_ref[...], weight[:, : 2 * width], 1, 0) + bias_ref[:, : 2 * width]
    pair = pair.astype(LOW)
    query = contract(normed_ref[:rows, :], weight[:, 2 * width :], 1, 0) + bias_ref[:, 2 * width :]
    query = (query.astype(LOW).astype(FULL) * HEAD_DIM**-0.5).astype(LOW)
    for head in range(heads):
        at = head * HEAD_DIM
        q_ref[head] = jnp.where(lane_q < HEAD_DIM, spread(query, width + at), ext_q_ref[...])
        k_ref[head] = jnp.where(lane_k < HEAD_DIM, spread(pair, at), ext_k)
        v_ref[head] = jnp.where(lane_k < HEAD_DIM, spread(pair, width + at), ext_k)
    saves = [
        pltpu.make_async_copy(source, target, leaving.at[at])
        for at, (source, target) in enumerate(
            ((k_ref, k_out), (v_ref, v_out), (q_ref, q_out), (mixed_ref, mixed_out))
        )
    ]
    saves[0].start()
    saves[1].start()
    for head in range(heads):
        scores = contract(q_ref[head], k_ref[head], 1, 1)
        highest = jnp.max(scores, axis=1, keepdims=True)
        weights = jnp.exp(scores - highest)
        total = jnp.sum(weights, axis=1, keepdims=True)
        mixed = contract(weights.astype(LOW), v_ref[head], 1, 0) / total
        mixed_ref[:, head * HEAD_DIM : (head + 1) * HEAD_DIM] = mixed[:, :HEAD_DIM].astype(LOW)
        pieces = pieces_of(-(highest + jnp.log(total)))
        q_ref[head] = put_pieces(lane_q, HEAD_DIM, pieces, q_ref[head])
    saves[2].start()
    saves[3].start()
    answer = contract(mixed_ref[...], weight[:, 2 * width : 3 * width], 1, 1)
    out_ref[...] = acc_ref[...] + answer if started else answer
    for save in saves:
        save.wait()


def attend(normed, source, bias, ext_q, ext_k, acc, heads):
    arrays, pieces = source
    rows, keys = ext_q.shape[0], ext_k.shape[0]
    model = normed.shape[1]
    saved = [
        ((rows, heads * HEAD_DIM), LOW),
        ((heads, rows, LANES), LOW),
        ((heads, keys, LANES), LOW),
        ((heads, keys, LANES), LOW),
    ]

    def kernel(*refs):
        attend_kernel(heads, rows, keys, pieces, acc is not None, *refs)

    start = [] if acc is None else [acc]
    return pl.pallas_call(
        kernel,
        out_shape=(
            jax.ShapeDtypeStruct((rows, model), FULL),
            *(pltpu.HBM(*item) for item in saved),
        ),
        in_specs=[WHOLE] * (4 + len(start)) + [ANYWHERE] * len(arrays),
        out_specs=(WHOLE,) + (ANYWHERE,) * 4,
        input_output_aliases={4: 0} if start else {},
        scratch_shapes=[
            pltpu.VMEM((model, arrays[0].shape[1]), LOW),
            *(pltpu.VMEM(*item) for item in saved),
            pltpu.SemaphoreType.DMA((len(pieces),)),
            pltpu.SemaphoreType.DMA((4,)),
        ],
        cost_estimate=pl.CostEstimate(
            flops=4 * heads * rows * keys * LANES + 8 * rows * model * heads * HEAD_DIM,
            transcendentals=heads * rows * keys,
            bytes_accessed=2 * (normed.size + 4 * rows * model + 8 * rows * heads * LANES),
        ),
        compiler_params=pltpu.CompilerParams(vmem_limit_bytes=14 << 20),
        name="attend",
    )(normed, bias, ext_q, ext_k, *start, *outside(arrays))


def mlp_kernel(
    block, pieces, place, started, finished,
    normed_ref, normed_t_ref, seed_ref, seed_t_ref, bias_ref, *refs
):
    if started:
        out_in_ref, d_in_ref, *refs = refs
    if finished:
        middle_ref, norm_ref, shuffle_ref, *refs = refs
        *refs, out_ref, d_ref = refs
        final = refs[-13:-8]
    else:
        out_ref, d_ref = refs[-10:-8]
    kept_out, sent_out, sums_ref = refs[-8:-5]
    weight, kept_ref, sent_ref, semaphores, leaving = refs[-5:]
    cut = kept_ref.shape[0]
    units = bias_ref.shape[1]

    def spans(at):
        return (
            pl.ds(pl.multiple_of(at * block, block), block),
            pl.ds(pl.multiple_of(units + at * block, block), block),
        )

    def copies(at):
        return [
            pltpu.make_async_copy(
                refs[source].at[pl.ds(start, count), span],
                weight.at[pl.ds(put, count), span],
                semaphores.at[at, 2 * order + side],
            )
            for order, (source, start, put, count) in enumerate(pieces)
            for side, span in enumerate(spans(at))
        ]

    def saves(at):
        return [
            pltpu.make_async_copy(
                source.at[:, span], target.at[place, :, span], leaving.at[at, 2 * order + side]
            )
            for order, (source, target) in enumerate(((kept_ref, kept_out), (sent_ref, sent_out)))
            for side, span in enumerate(spans(at))
        ]

    for at in range(units // block):
        for copy in copies(at):
            copy.start()
    out_ref[...] = out_in_ref[...] if started else jnp.zeros(out_ref.shape, FULL)
    d_ref[...] = d_in_ref[...] if started else jnp.zeros(d_ref.shape, FULL)

    def step(at, carry):
        span_up, span_down = spans(at)
        for copy in copies(at):
            copy.wait()
        up = contract(normed_ref[...], weight[:, span_up], 1, 0) + bias_ref[:, span_up]
        d_active = contract(seed_ref[...], weight[:, span_down], 1, 0)
        cumulative = 0.5 + 0.5 * lax.erf(up * 0.7071067811865476)
        active = (up * cumulative).astype(LOW)
        slope = cumulative + up * (jnp.exp(-0.5 * up * up) * 0.3989422804014327)
        d_up = (d_active * slope).astype(LOW)
        sums_ref[:, span_up] = jnp.sum(d_up.astype(FULL), axis=0, keepdims=True)
        out_ref[...] += contract(active, weight[:, span_down], 1, 1)
        d_ref[...] += contract(d_up, weight[:, span_up], 1, 1)
        grad_up = contract(normed_t_ref[...], d_up, 1, 0).astype(LOW)
        kept_ref[:, span_up] = grad_up[:cut]
        sent_ref[:, span_up] = grad_up[cut:]
        grad_down = contract(seed_t_ref[...], active, 1, 0).astype(LOW)
        kept_ref[:, span_down] = grad_down[:cut]
        sent_ref[:, span_down] = grad_down[cut:]
        for save in saves(at):
            save.start()
        return carry

    lax.fori_loop(0, units // block, step, 0)
    if finished:
        second_back_kernel(middle_ref, d_ref, seed_ref, out_ref, norm_ref, shuffle_ref, *final)
    for at in range(units // block):
        for save in saves(at):
            save.wait()


def mlp(normed, normed_t, seed, seed_t, source, bias, out, d_normed, grads, at, total, finish):
    arrays, pieces = source
    rows, model = normed.shape
    units = bias.shape[1]
    cut = model // 2

    def kernel(*refs):
        mlp_kernel(256, pieces, at, out is not None, bool(finish), *refs)

    grad_shape = pltpu.HBM((total, cut, 2 * units), LOW)
    grads = list(grads)
    start = [] if out is None else [out, d_normed]
    first = 5 + len(start) + len(finish) + len(arrays)
    tall, wide = (rows, model), (model, rows)
    leading = [(tall, FULL), (tall, FULL)]
    if finish:
        leading = [(tall, FULL), (tall, LOW), (wide, LOW), (tall, LOW), ((4, model), FULL)]
    lead = len(leading)
    return pl.pallas_call(
        kernel,
        out_shape=(
            *(jax.ShapeDtypeStruct(*shape) for shape in leading),
            grad_shape,
            grad_shape,
            jax.ShapeDtypeStruct((1, units), FULL),
        ),
        in_specs=[WHOLE] * (5 + len(start) + len(finish))
        + [ANYWHERE] * (len(arrays) + len(grads)),
        out_specs=(*(WHOLE,) * lead, ANYWHERE, ANYWHERE, WHOLE),
        input_output_aliases={
            **({5: 0, 6: 1} if start and not finish else {}),
            **({first: lead, first + 1: lead + 1} if grads else {}),
        },
        scratch_shapes=[
            pltpu.VMEM((model, 2 * units), LOW),
            pltpu.VMEM((cut, 2 * units), LOW),
            pltpu.VMEM((cut, 2 * units), LOW),
            pltpu.SemaphoreType.DMA((units // 256, 2 * len(pieces))),
            pltpu.SemaphoreType.DMA((units // 256, 4)),
            *([pltpu.VMEM(tall, FULL)] * 2 if finish else []),
        ],
        cost_estimate=pl.CostEstimate(
            flops=12 * rows * model * units,
            transcendentals=2 * rows * units,
            bytes_accessed=16 * rows * model + 8 * model * units,
        ),
        compiler_params=pltpu.CompilerParams(vmem_limit_bytes=(24 if finish else 14) << 20),
        name="mlp",
    )(normed, normed_t, seed, seed_t, bias, *start, *finish, *outside(arrays), *outside(grads))


def back_kernel(
    heads, rows, keys, pieces, started, d_ref, d_t_ref, normed_t_ref, *refs
):
    if started:
        own_in_ref, other_in_ref, *refs = refs
    q_in, k_in, v_in, mixed_in, *refs = refs
    own_ref, other_ref, kept_out, sent_out, sums_ref = refs[-19:-14]
    (
        weight, q_ref, k_ref, v_ref, mixed_ref, kept_ref, sent_ref,
        u_buf, dq_buf, dk_buf, dv_buf, pair_buf, query_buf, semaphores,
    ) = refs[-14:]
    width = heads * HEAD_DIM
    cut = kept_ref.shape[0]
    first = len(pieces)
    entering = [
        pltpu.make_async_copy(source, target, semaphores.at[first + at])
        for at, (source, target) in enumerate(
            ((mixed_in, mixed_ref), (q_in, q_ref), (k_in, k_ref), (v_in, v_ref))
        )
    ]
    for copy in entering:
        copy.start()
    fetch(pieces, refs, weight, semaphores)
    lane_q = lane_of(rows)
    upstream_all = contract(d_ref[...], weight[:, 2 * width : 3 * width], 1, 0).astype(LOW)
    entering[0].wait()
    mixed = mixed_ref[...]
    for head in range(heads):
        at = head * HEAD_DIM
        product = upstream_all[:, at : at + HEAD_DIM].astype(FULL) * mixed[
            :, at : at + HEAD_DIM
        ].astype(FULL)
        pieces_here = pieces_of(-jnp.sum(product, axis=1, keepdims=True))
        rest = jnp.where(lane_q < HEAD_DIM, spread(upstream_all, at), jnp.zeros((), LOW))
        u_buf[head] = put_pieces(lane_q, HEAD_DIM, pieces_here, rest)
    for copy in entering[1:]:
        copy.wait()
    block = 256

    def one_head(head, carry):
        queries = q_ref[head]
        upstream = u_buf[head]
        total = jnp.zeros((rows, LANES), FULL)
        for start in range(0, keys, block):
            span = pl.ds(start, block)
            keys_part = k_ref[head, span, :]
            shares = jnp.exp(contract(keys_part, queries, 1, 1))
            d_scores = (shares * contract(v_ref[head, span, :], upstream, 1, 1)).astype(LOW)
            dv_buf[head, span, :] = contract(shares.astype(LOW), upstream, 1, 0).astype(LOW)
            dk_buf[head, span, :] = contract(d_scores, queries, 1, 0).astype(LOW)
            total = total + contract(d_scores, keys_part, 0, 0)
        dq_buf[head] = (total * HEAD_DIM**-0.5).astype(LOW)
        return carry

    lax.fori_loop(0, heads, one_head, 0)
    query_buf[:, :width] = jnp.zeros((rows, width), LOW)
    for head in range(heads):
        at = head * HEAD_DIM
        query_buf[:, width + at : width + at + HEAD_DIM] = dq_buf[head][:, :HEAD_DIM]
        pair_buf[:, at : at + HEAD_DIM] = dk_buf[head][:, :HEAD_DIM]
        pair_buf[:, width + at : width + at + HEAD_DIM] = dv_buf[head][:, :HEAD_DIM]
    grad_pair = contract(normed_t_ref[...], pair_buf[...], 1, 0).astype(LOW)
    kept_ref[:, : 2 * width] = grad_pair[:cut]
    sent_ref[:, : 2 * width] = grad_pair[cut:]
    grad_query = contract(normed_t_ref[:, :rows], query_buf[...], 1, 0).astype(LOW)
    kept_ref[:, 2 * width :] = grad_query[:cut]
    sent_ref[:, 2 * width :] = grad_query[cut:]
    grad_out = contract(d_t_ref[...], mixed, 1, 0).astype(LOW)
    kept_ref[:, 2 * width : 3 * width] = grad_out[:cut]
    sent_ref[:, 2 * width : 3 * width] = grad_out[cut:]
    saves = [
        pltpu.make_async_copy(kept_ref, kept_out, semaphores.at[first + 4]),
        pltpu.make_async_copy(sent_ref, sent_out, semaphores.at[first + 5]),
    ]
    for save in saves:
        save.start()
    sums_ref[:, : 2 * width] = jnp.sum(pair_buf[...].astype(FULL), axis=0, keepdims=True)
    sums_ref[:, 2 * width :] = jnp.sum(query_buf[...].astype(FULL), axis=0, keepdims=True)
    own = contract(pair_buf[:rows, :], weight[:, : 2 * width], 1, 1) + contract(
        query_buf[...], weight[:, 2 * width :], 1, 1
    )
    own_ref[...] = own_in_ref[...] + own if started else own
    other = contract(pair_buf[rows:, :], weight[:, : 2 * width], 1, 1)
    other_ref[...] = (other_in_ref[...] + other if started else other).astype(other_ref.dtype)
    for save in saves:
        save.wait()


def attend_back(d_middle, d_middle_t, normed_t, source, saved, own, other, heads, last):
    arrays, pieces = source
    mixed, queries, keys_all, values = saved
    rows, keys = d_middle.shape[0], normed_t.shape[1]
    model = normed_t.shape[0]
    cut, columns = model // 2, arrays[0].shape[1]
    width = heads * HEAD_DIM

    def kernel(*refs):
        back_kernel(heads, rows, keys, pieces, own is not None, *refs)

    start = [] if own is None else [own, other]
    aliases = {3: 0, 4: 1} if start else {}
    if last:
        aliases.pop(4)
    return pl.pallas_call(
        kernel,
        out_shape=(
            jax.ShapeDtypeStruct((rows, model), FULL),
            jax.ShapeDtypeStruct((rows, model), LOW if last else FULL),
            pltpu.HBM((cut, columns), LOW),
            pltpu.HBM((cut, columns), LOW),
            jax.ShapeDtypeStruct((1, columns), FULL),
        ),
        in_specs=[WHOLE] * (3 + len(start)) + [ANYWHERE] * (4 + len(arrays)),
        out_specs=(WHOLE, WHOLE, ANYWHERE, ANYWHERE, WHOLE),
        input_output_aliases=aliases,
        scratch_shapes=[
            pltpu.VMEM((model, columns), LOW),
            pltpu.VMEM((heads, rows, LANES), LOW),
            pltpu.VMEM((heads, keys, LANES), LOW),
            pltpu.VMEM((heads, keys, LANES), LOW),
            pltpu.VMEM((rows, width), LOW),
            pltpu.VMEM((cut, columns), LOW),
            pltpu.VMEM((cut, columns), LOW),
            pltpu.VMEM((heads, rows, LANES), LOW),
            pltpu.VMEM((heads, rows, LANES), LOW),
            pltpu.VMEM((heads, keys, LANES), LOW),
            pltpu.VMEM((heads, keys, LANES), LOW),
            pltpu.VMEM((keys, 2 * width), LOW),
            pltpu.VMEM((rows, columns - 2 * width), LOW),
            pltpu.SemaphoreType.DMA((len(pieces) + 6,)),
        ],
        cost_estimate=pl.CostEstimate(
            flops=10 * heads * rows * keys * LANES + 20 * rows * model * width,
            transcendentals=heads * rows * keys,
            bytes_accessed=8 * keys * model + 8 * rows * model,
        ),
        compiler_params=pltpu.CompilerParams(vmem_limit_bytes=16 << 20),
        name="attend_back",
    )(
        d_middle, d_middle_t, normed_t, *start,
        *outside((queries, keys_all, values, mixed)), *outside(arrays),
    )


def call_rows(kernel, shapes, *arrays):
    return pl.pallas_call(
        kernel,
        out_shape=tuple(jax.ShapeDtypeStruct(*shape) for shape in shapes),
        in_specs=[WHOLE] * len(arrays),
        out_specs=(WHOLE,) * len(shapes),
        cost_estimate=pl.CostEstimate(
            flops=2 * arrays[0].size * arrays[0].shape[1],
            transcendentals=0,
            bytes_accessed=sum(array.size * array.dtype.itemsize for array in arrays),
        ),
        compiler_params=pltpu.CompilerParams(vmem_limit_bytes=12 << 20),
    )(*arrays)


def pack_kernel(
    rows, spots_ref, gains_ref, shifts_ref, heads_ref, ups_ref, labels_ref, out_ref, line
):
    at = 0
    for ref in (gains_ref, shifts_ref, heads_ref, ups_ref):
        count, size = ref.shape
        for which in range(count):
            line[:, at : at + size] = ref[which : which + 1, :].astype(FULL)
            at += size
    start = pl.multiple_of(spots_ref[2], LANES)
    line[:, at:] = labels_ref[pl.ds(spots_ref[1], 1), pl.ds(start, rows)].astype(FULL)
    place = lax.broadcasted_iota(jnp.int32, out_ref.shape, 0) == spots_ref[0]
    out_ref[...] = jnp.where(place, jnp.broadcast_to(line[...], out_ref.shape), 0.0).astype(LOW)


def pack_small(spots, devices, rows, *arrays):
    size = sum(array.size for array in arrays[:-1]) + rows

    def kernel(*refs):
        pack_kernel(rows, *refs)

    return pl.pallas_call(
        kernel,
        out_shape=jax.ShapeDtypeStruct((devices, size), LOW),
        in_specs=[pl.BlockSpec(memory_space=pltpu.SMEM)] + [WHOLE] * len(arrays),
        out_specs=WHOLE,
        scratch_shapes=[pltpu.VMEM((1, size), FULL)],
        compiler_params=pltpu.CompilerParams(vmem_limit_bytes=4 << 20),
        name="pack_small",
    )(spots, *arrays)


def pick_kernel(starts_ref, sums_ref, gains_ref, shifts_ref, heads_ref, ups_ref):
    total = sums_ref.shape[1]

    def window(first, count, which, size):
        moved = pltpu.roll(sums_ref[...], (total - starts_ref[which]) % total, 1)
        return moved[first : first + count, :size]

    fine, piece, unit = gains_ref.shape[1], heads_ref.shape[1], ups_ref.shape[1]
    gains_ref[...] = window(0, 2, 0, fine)
    shifts_ref[...] = window(2, 4, 0, fine)
    heads_ref[0:1, :] = window(6, 1, 2, piece)
    heads_ref[1:2, :] = window(6, 1, 1, piece)
    ups_ref[...] = window(7, 1, 3, unit)


def pick_own(starts, sums, fine, piece, unit):
    return pl.pallas_call(
        pick_kernel,
        out_shape=tuple(
            jax.ShapeDtypeStruct(shape, FULL)
            for shape in ((2, fine), (4, fine), (2, piece), (1, unit))
        ),
        in_specs=[pl.BlockSpec(memory_space=pltpu.SMEM), WHOLE],
        compiler_params=pltpu.CompilerParams(vmem_limit_bytes=4 << 20),
        name="pick_own",
    )(starts, sums)


def enter_kernel(rows_ref, shuffle_ref, out_ref, out_t_ref):
    moved = contract(rows_ref[...], shuffle_ref[...], 1, 0).astype(LOW)
    out_ref[...] = moved
    out_t_ref[...] = moved.T


def first_norm_kernel(rows_ref, shuffle_ref, norm_ref, rows_out, normed_ref):
    moved = contract(rows_ref[...], shuffle_ref[...], 1, 0)
    rows_out[...] = moved.astype(LOW)
    normed_ref[...] = normalize(moved, norm_ref[0:1, :], norm_ref[2:3, :])[0].astype(LOW)


def both_kernel(own_ref, other_ref, both_ref, both_t_ref):
    rows, model = own_ref.shape
    cut = model // 2
    both_ref[:rows, :] = own_ref[...]
    both_ref[rows:, :cut] = other_ref[:, cut:]
    both_ref[rows:, cut:] = other_ref[:, :cut]
    both_t_ref[...] = both_ref[...].T


def second_norm_kernel(rows_ref, attended_ref, norm_ref, middle_ref, normed_ref, normed_t_ref):
    middle = rows_ref[...].astype(FULL) + attended_ref[...] + norm_ref[4:5, :]
    middle_ref[...] = middle
    normed = normalize(middle, norm_ref[1:2, :], norm_ref[3:4, :])[0].astype(LOW)
    normed_ref[...] = normed
    normed_t_ref[...] = normed.T


def add_up(array):
    return jnp.sum(array, axis=0, keepdims=True)


def second_back_kernel(
    middle_ref, d_normed_ref, seed_ref, mlp_ref, norm_ref, shuffle_ref,
    d_ref, d_low_ref, d_t_ref, result_ref, sums_ref,
):
    middle = middle_ref[...]
    _, unit, inverse = normalize(middle, norm_ref[1:2, :], norm_ref[3:4, :])
    d_normed = d_normed_ref[...]
    seed = seed_ref[...].astype(FULL)
    d_middle = seed + norm_back(d_normed, unit, inverse, norm_ref[1:2, :])
    d_ref[...] = d_middle
    low = d_middle.astype(LOW)
    d_low_ref[...] = low
    d_t_ref[...] = low.T
    sums_ref[0:1, :] = add_up(d_normed * unit)
    sums_ref[1:2, :] = add_up(d_normed)
    sums_ref[2:3, :] = add_up(d_middle)
    sums_ref[3:4, :] = add_up(seed)
    result = (middle + mlp_ref[...] + norm_ref[5:6, :]).astype(LOW)
    result_ref[...] = contract(result, shuffle_ref[...], 1, 1).astype(LOW)


def first_back_kernel(
    rows_ref, own_ref, other_ref, d_middle_ref, norm_ref, shuffle_ref, d_rows_ref, sums_ref
):
    cut = own_ref.shape[1] // 2
    _, unit, inverse = normalize(rows_ref[...].astype(FULL), norm_ref[0:1, :], norm_ref[2:3, :])
    other = jnp.concatenate([other_ref[:, cut:], other_ref[:, :cut]], axis=1)
    d_normed = own_ref[...] + other.astype(FULL)
    d_rows = d_middle_ref[...] + norm_back(d_normed, unit, inverse, norm_ref[0:1, :])
    d_rows_ref[...] = contract(d_rows.astype(LOW), shuffle_ref[...], 1, 1).astype(LOW)
    sums_ref[0:1, :] = add_up(d_normed * unit)
    sums_ref[1:2, :] = add_up(d_normed)


def build(fsdp, tp):
    bits = fsdp.bit_length() - 1
    tp_bits = tp.bit_length() - 1
    masks = sorted(range(fsdp), key=lambda mask: (mask & 1, mask >> 1))

    def flip(array, bit):
        return lax.ppermute(array, "fsdp", [(at, at ^ (1 << bit)) for at in range(fsdp)])

    def flip_tp(array, bit):
        return lax.ppermute(array, "tp", [(at, at ^ (1 << bit)) for at in range(tp)])

    def trade_rows(array):
        pairs = []
        for row in range(fsdp):
            for column in range(tp):
                odd = (row ^ column) & 1
                pairs.append((row * tp + column, (row ^ odd) * tp + (column ^ odd)))
        return lax.ppermute(array, ("fsdp", "tp"), pairs)

    def sum_everywhere(array):
        for bit in range(bits):
            arrived = flip(array, bit)
            array = array + arrived
        for bit in range(tp_bits):
            arrived = flip_tp(array, bit)
            array = array + arrived
        return array

    def order_of(slot):
        upper = list(range(1, bits))
        return upper if slot % 2 == 0 else upper[::-1]

    def gather_rows(current, count, turn):
        rows = current.shape[0] // count
        order = order_of(turn)
        held = [(0, at) for at in range(count)]
        for bit in order[:-1]:
            both = held + [(mask ^ (1 << bit), at) for mask, at in held]
            arrived = flip(current, bit)
            current, held = join([current, arrived]), both
        last = order[-1]
        arrived = flip(current, last)
        found = [(current, held), (arrived, [(mask ^ (1 << last), at) for mask, at in held])]
        if rows % 16:
            wanted = sorted(found[0][1] + found[1][1], key=lambda item: (item[1], item[0]))
            cut = {}
            for array, items in found:
                for spot, item in enumerate(items):
                    cut[item] = array[spot * rows : (spot + 1) * rows]
            found = [(jnp.concatenate([cut[item] for item in wanted], axis=0), wanted)]
        found += [(flip(array, 0), [(mask ^ 1, at) for mask, at in items]) for array, items in found]
        arrays = [array for array, _ in found]
        sources = []
        for at in range(count):
            pieces = []
            for index, (_, items) in enumerate(found):
                for spot, (mask, shard) in enumerate(items):
                    if shard != at:
                        continue
                    start, put = spot * rows, masks.index(mask) * rows
                    if pieces:
                        source, before, place, length = pieces[-1]
                        if (source, before + length, place + length) == (index, start, put):
                            pieces[-1] = (source, before, place, length + rows)
                            continue
                    pieces.append((index, start, put, rows))
            sources.append((arrays, pieces))
        return sources

    def scatter_rows(kept, sent, turn):
        arrived = flip(sent, 0)
        terms = [kept, arrived]
        held = [mask for mask in masks if not mask & 1]
        rows = kept.shape[-2] // len(held)

        def pick(array, positions):
            if positions == list(range(positions[0], positions[0] + len(positions))):
                return array[..., positions[0] * rows : (positions[-1] + 1) * rows, :]
            return jnp.concatenate(
                [array[..., at * rows : (at + 1) * rows, :] for at in positions], axis=-2
            )

        for bit in order_of(turn)[::-1]:
            stay = [at for at, mask in enumerate(held) if not mask >> bit & 1]
            leave = [at for at, mask in enumerate(held) if mask >> bit & 1]
            leaving = total_of([pick(term, leave) for term in terms]).astype(LOW)
            arrived = flip(leaving, bit)
            terms = [pick(term, stay) for term in terms] + [arrived]
            held = [held[at] for at in stay]
        return terms

    def spread_tp(shard):
        slots = [shard]
        for bit in range(tp_bits):
            for at in range(1 << bit):
                slots.append(flip_tp(slots[at], bit))
        return slots

    def local(
        frames, segments, w_qkv, w_out, w_up, w_down, head_bias, up_bias, ln_gains, shifts, cotangent
    ):
        row = lax.axis_index("fsdp")
        column = lax.axis_index("tp")
        rows, model = frames.shape
        block = model // fsdp
        width = w_qkv.shape[2]
        heads = width // HEAD_DIM
        units = w_up.shape[1]
        fine = ln_gains.shape[1]

        parts = [w_qkv[:, 1], w_qkv[:, 2], w_out.T, w_qkv[:, 0]]
        first_shard = jnp.concatenate(parts, axis=1)
        second_shard = jnp.concatenate([w_up, w_down.T], axis=1)
        first_parts = spread_tp(first_shard)
        pairs = [join(first_parts[at : at + 2]) for at in range(0, tp, 2)]
        first_slots = []
        for at, pair in enumerate(pairs):
            first_slots += gather_rows(pair, 2, at)
        second_slots = []
        for slot, shard in enumerate(spread_tp(second_shard)):
            second_slots += gather_rows(shard, 1, min(slot, 1))

        here = tp // segments.shape[0]
        spots = jnp.stack([row * tp + column, column // here, column % here * rows])
        small = sum_everywhere(
            pack_small(
                spots, fsdp * tp, rows,
                ln_gains, shifts, head_bias, up_bias.reshape(1, -1), segments,
            )
        )
        cut = 6 * fine
        norm_rows = small[:, :cut].reshape(fsdp * tp, 6, fine).transpose(1, 0, 2).reshape(6, model)
        piece = head_bias.shape[1]
        head_rows = small[:, cut : cut + 2 * piece].reshape(fsdp, tp, 2, piece)
        head_rows = head_rows.transpose(1, 2, 0, 3).reshape(tp, 2, width).astype(FULL)
        up_rows = small[:, cut + 2 * piece : -rows].reshape(fsdp, tp, up_bias.shape[0])
        up_rows = up_rows.transpose(1, 0, 2).reshape(tp, 1, units).astype(FULL)

        out_at = lax.broadcasted_iota(jnp.int32, (model, model), 1)
        in_at = lax.broadcasted_iota(jnp.int32, (model, model), 0)
        spot = out_at // block
        mask_at = ((spot & (fsdp // 2 - 1)) << 1) | (spot >> (bits - 1))
        shuffle = (in_at == (row ^ mask_at) * block + out_at % block).astype(LOW)

        norm_rows = contract(norm_rows, shuffle, 1, 0)
        first_row = ((row & -2) | (column & 1)) * tp + (column & -2)

        def labels_of(half):
            found = lax.dynamic_index_in_dim(small, first_row + half, 0, keepdims=False)
            return found[-rows:].astype(jnp.int32)

        own_labels, other_labels = labels_of(row & 1), labels_of(1 - (row & 1))
        all_labels = jnp.concatenate([own_labels, other_labels])

        def extension(labels_part, lead, marks):
            lane = lane_of(labels_part.shape[0])
            clip = lane - (HEAD_DIM + 3)
            values = jnp.where((clip >= 0) & (clip < CLIPS), marks(clip == labels_part[:, None]), 0.0)
            is_lead = (lane >= HEAD_DIM) & (lane < HEAD_DIM + 3)
            return jnp.where(is_lead, lead, values).astype(LOW)

        ext_q = extension(own_labels, 0.0, lambda same: jnp.where(same, 0.0, MASKED))
        ext_k = extension(all_labels, 1.0, lambda same: jnp.where(same, 1.0, 0.0))

        tall = (rows, model)
        wide = (model, rows)
        local_rows, first_low = call_rows(
            first_norm_kernel, ((tall, LOW), (tall, LOW)),
            trade_rows(frames), shuffle, norm_rows,
        )
        first_both, first_t = call_rows(
            both_kernel, (((2 * rows, model), LOW), ((model, 2 * rows), LOW)),
            first_low, flip(first_low, 0),
        )
        seed = trade_rows(cotangent)
        upstream_low, upstream_t = call_rows(
            enter_kernel, ((tall, LOW), (wide, LOW)), seed, shuffle
        )

        def slot_row(array, slot):
            return lax.dynamic_index_in_dim(array, column ^ slot, 0, keepdims=False)

        saved = []
        attended = None
        none = jnp.zeros((width,), FULL)
        for slot in range(tp):
            bias = slot_row(head_rows, slot)
            bias = jnp.concatenate([none, bias[1], none, bias[0]])[None]
            attended, *kept = attend(
                first_both, first_slots[slot], bias, ext_q, ext_k, attended, heads
            )
            saved.append(kept)
        middle, second_low, second_t = call_rows(
            second_norm_kernel, ((tall, FULL), (tall, LOW), (wide, LOW)),
            local_rows, attended, norm_rows,
        )

        answers = (None, None)
        grad_second, unit_sums, grads = [], [], ()
        for slot in range(tp):
            *answers, kept, sent, sums = mlp(
                second_low, second_t, upstream_low, upstream_t, second_slots[slot],
                slot_row(up_rows, slot), *answers, grads, slot % 2, 2,
                (middle, norm_rows, shuffle) if slot == tp - 1 else (),
            )
            grads = (kept, sent)
            unit_sums.append(sums)
            if slot % 2:
                grad_second.append(scatter_rows(*grads, slot // 2))
                grads = ()
        d_middle, d_middle_low, d_middle_t, result, early_sums = answers
        result = trade_rows(result)

        def sum_tp(parts):
            for bit in range(tp_bits):
                for slot in range(tp - (1 << bit), 0, -(2 << bit)):
                    arrived = flip_tp(total_of(parts[slot]).astype(LOW), bit)
                    parts[slot ^ (1 << bit)] = parts[slot ^ (1 << bit)] + [arrived]
            return total_of(parts[0])

        grad_first = [None] * tp
        head_sums = [None] * tp
        d_own = d_other = None
        for slot in range(tp - 1, -1, -1):
            d_own, d_other, kept, sent, sums = attend_back(
                d_middle_low, d_middle_t, first_t, first_slots[slot], saved[slot],
                d_own, d_other, heads, slot == 0,
            )
            grad_first[slot] = scatter_rows(kept, sent, slot)
            head_sums[slot] = sums
        d_rows, late_sums = call_rows(
            first_back_kernel, ((tall, LOW), ((2, model), FULL)),
            local_rows, d_own, flip(d_other, 0), d_middle, norm_rows, shuffle,
        )
        d_rows = trade_rows(d_rows)

        sums = jnp.concatenate(
            [late_sums[:1], early_sums[:1], late_sums[1:], early_sums[1:]], axis=0
        )
        sums = lax.dot_general(
            sums,
            shuffle.astype(FULL),
            (((1,), (1,)), ((), ())),
            precision=lax.Precision.HIGHEST,
            preferred_element_type=FULL,
        )
        packed = jnp.concatenate(
            [sums] + [item for pair in zip(head_sums, unit_sums) for item in pair], axis=0
        )
        for bit in range(bits):
            arrived = flip(packed, bit)
            packed = packed + arrived
        for bit in range(tp_bits - 1, -1, -1):
            keep = 6 + 2 * (1 << bit)
            arrived = flip_tp(jnp.concatenate([packed[:6], packed[keep:]], axis=0), bit)
            packed = packed[:keep] + arrived
        starts = jnp.stack(
            [(row * tp + column) * fine, width + row * piece, 3 * width + row * piece, row * up_bias.shape[0]]
        )
        gain_grads, shift_grads, grad_headbias, grad_upbias = pick_own(
            starts, packed, fine, piece, up_bias.shape[0]
        )
        grad_upbias = grad_upbias[0]

        total_first = sum_tp(grad_first)
        total_second = sum_tp([[term[at % 2] for term in grad_second[at // 2]] for at in range(tp)])
        total_qkv = [total_first[:, at * width : (at + 1) * width] for at in (3, 0, 1)]
        return (
            result,
            d_rows,
            jnp.stack(total_qkv, axis=1),
            total_first[:, 2 * width : 3 * width].T,
            total_second[:, :units],
            total_second[:, units:].T,
            grad_headbias,
            grad_upbias,
            gain_grads,
            shift_grads,
        )

    return local


def solution(mesh):
    placed = (
        P(("fsdp", "tp"), None),
        P("fsdp", None),
        P("fsdp", None, "tp"),
        P("tp", "fsdp"),
        P("fsdp", "tp"),
        P("tp", "fsdp"),
        P(None, ("tp", "fsdp")),
        P(("tp", "fsdp")),
        P(None, ("fsdp", "tp")),
        P(None, ("fsdp", "tp")),
        P(("fsdp", "tp"), None),
    )
    body = build(mesh.shape["fsdp"], mesh.shape["tp"])

    return jax.shard_map(
        body,
        mesh=mesh,
        in_specs=placed,
        out_specs=(
            P(("fsdp", "tp"), None),
            P(("fsdp", "tp"), None),
            P("fsdp", None, "tp"),
            P("tp", "fsdp"),
            P("fsdp", "tp"),
            P("tp", "fsdp"),
            P(None, ("tp", "fsdp")),
            P(("tp", "fsdp")),
            P(None, ("fsdp", "tp")),
            P(None, ("fsdp", "tp")),
        ),
        check_vma=False,
    )
```
